32 devices in a mesh: tm: 16 (over z, x, core), grid: 2 (over y).
Axes of the slice: x: 2, y: 2, z: 4, core: 2. Of those that a mesh axis runs over, the one named last changes fastest.
Arguments:
- times: float32 [8192], P(('tm', 'grid')), as said below
- cell_row: int32 [8192], P(('tm', 'grid')), may hold values from 0 to 127
- cell_col: int32 [8192], P(('tm', 'grid')), may hold values from 0 to 16383
- magnitude: int32 [8192], P(('tm', 'grid')), may hold values from 0 to 7
- base_rate: float32 [8192], P(('tm', 'grid')), may hold values from 0.02 to 0.2
- productivity: float32 [8], replicated, may hold values from 0.05 to 5
- spread: float32 [8], replicated, may hold values from 0.8 to 4.8
Outputs:
- log_event_intensity: float32 [8192], P(('tm', 'grid'))
- density: float32 [128, 16384], P(('tm', 'grid'))
The draws below stay inside these ranges and needn't reach their ends.
Inputs may be any that keep to these rules, and one draw needn't show every extreme that they name: `times`: never decreasing along the events.
All inputs are finite; a program needn't handle non-finite values.
Results may differ from the reference program's by a relative error of at most 0.003.
Values sent between devices are 32-bit elements; how exact they have to be, the bound alone decides.
No kernel may reach another device: no remote copies, remote signals or barrier semaphores. Data moves between devices by JAX's collectives and lax.ppermute only.
A program may use at most 64 MiB of HBM per device.

```python
import math
import jax
import jax.numpy as jnp
from jax import lax

BLOCK_EVENTS = 256
NB = 2
NBIN = 8
LATITUDE_SPAN = 4
COLS = 16384
EVENT_TOTAL = 8192
ROWS = 128


def event_cells(key):
    folded = jax.random.fold_in(key, 11)
    split_random_keys = jax.random.split(folded, 8)
    site_count = max(4, BLOCK_EVENTS // 16)
    reach_cells = 48
    block_count = EVENT_TOTAL // BLOCK_EVENTS
    holder_count = ROWS // LATITUDE_SPAN
    site_rows = jax.random.randint(split_random_keys[0], (site_count,), 0, ROWS)
    site_cols = jax.random.randint(split_random_keys[1], (site_count,), 0, COLS)
    chosen = jax.random.randint(split_random_keys[2], (EVENT_TOTAL,), 0, site_count)
    row_shift = jax.random.randint(split_random_keys[3], (EVENT_TOTAL,), -reach_cells, reach_cells + 1)
    col_shift = jax.random.randint(split_random_keys[4], (EVENT_TOTAL,), -reach_cells, reach_cells + 1)
    full_lattice_tile = jax.random.randint(split_random_keys[5], (), 1, block_count)
    full_lattice_store = jax.random.randint(split_random_keys[6], (), 0, holder_count)
    lattice_line_start = jax.random.randint(split_random_keys[7], (EVENT_TOTAL,), 0, LATITUDE_SPAN)
    lattice_breadth = (site_rows[chosen] + row_shift) % ROWS
    col_cells = (site_cols[chosen] + col_shift) % COLS
    quake_record_tile = jnp.arange(EVENT_TOTAL, dtype=jnp.int32) // BLOCK_EVENTS
    inside_cascade = quake_record_tile == full_lattice_tile
    lattice_breadth = jnp.where(inside_cascade, full_lattice_store * LATITUDE_SPAN + lattice_line_start, lattice_breadth)
    lattice_breadth = lattice_breadth.at[0].set(ROWS - 1).at[1].set(0)
    col_cells = col_cells.at[0].set(COLS - 1).at[1].set(0)
    return (lattice_breadth.astype(jnp.int32), col_cells.astype(jnp.int32))


def draw_cell_row(key, part):
    return event_cells(key)[0]


def draw_cell_col(key, part):
    return event_cells(key)[1]


def draw_times(key, part):
    split_random_keys = jax.random.split(jax.random.fold_in(key, 23), 2)
    grid_spacing = jax.random.exponential(split_random_keys[0], (EVENT_TOTAL,), jnp.float32)
    cluster_scale = jnp.exp(jax.random.uniform(split_random_keys[1], (EVENT_TOTAL,), jnp.float32, -2.0, 1.0))
    return (0.1 + jnp.cumsum(grid_spacing * cluster_scale / BLOCK_EVENTS)).astype(jnp.float32)


def set_ends(array, own_key, least, high):
    longest = array.shape.index(max(array.shape))
    spots = []
    for shift in (0, 1):
        where = [jax.random.randint(jax.random.fold_in(own_key, axis), (), 0, length) for axis, length in enumerate(array.shape)]
        where[longest] = (where[longest] + shift) % array.shape[longest]
        spots.append(tuple(where))
    return array.at[spots[0]].set(least).at[spots[1]].set(high)


def steps_of(key, dims, shards, smallest, high):
    def one(dim, blocks):
        heights = jax.random.uniform(jax.random.fold_in(jax.random.fold_in(key, 6), dim), (blocks,), jnp.float32, smallest / len(shards), high / len(shards))
        return jnp.repeat(jnp.exp(heights), dims[dim] // blocks).reshape((-1,) + (1,) * (len(dims) - dim - 1))

    gain = one(*shards[0])
    for cut in shards[1:]:
        gain = gain * one(*cut)
    return gain


def setup_inputs(seed: int = 0) -> dict:
    arg_keys = jax.random.split(jax.random.key(seed), 8)
    times = draw_times(jax.random.fold_in(arg_keys[7], 71), 0)
    cell_row = draw_cell_row(jax.random.fold_in(arg_keys[7], 71), 0)
    cell_col = draw_cell_col(jax.random.fold_in(arg_keys[7], 71), 0)
    magnitude = set_ends(jax.random.randint(arg_keys[3], (EVENT_TOTAL,), 0, NBIN), jax.random.fold_in(arg_keys[3], 1), 0, NBIN - 1).astype(jnp.int32)
    base_rate = jnp.clip(jnp.exp(math.log(0.2) - 2.3025851 * jax.random.uniform(arg_keys[4], (EVENT_TOTAL,), jnp.float32) ** steps_of(arg_keys[4], (EVENT_TOTAL,), ((0, 32),), -0.2, 0.2)), 0.02, 0.2)
    productivity = jnp.clip(jnp.exp(jax.random.uniform(arg_keys[5], (NBIN,), jnp.float32, math.log(0.05), math.log(5.0))), 0.05, 5.0)
    spread = jnp.clip(jnp.exp(jax.random.uniform(arg_keys[6], (NBIN,), jnp.float32, math.log(0.8), math.log(4.8))), 0.8, 4.8)
    return dict(times=times, cell_row=cell_row, cell_col=cell_col, magnitude=magnitude, base_rate=base_rate, productivity=productivity, spread=spread)


omori_power = 1.2
omori_offset = 0.5
cell_km = 0.1
smooth_sigma = 1.5
rim_width = 3


def event_terms(times, cell_row, cell_col, magnitude, productivity, spread):
    producing = productivity[magnitude]
    sigma_km = spread[magnitude]
    normalizing_factor = (omori_power - 1.0) * omori_offset ** (omori_power - 1.0)
    amplitude = producing * normalizing_factor / (2.0 * math.pi * sigma_km * sigma_km)
    inverse = 1.0 / (2.0 * sigma_km * sigma_km)
    return jnp.stack([times, cell_row.astype(jnp.float32), cell_col.astype(jnp.float32), amplitude, inverse])


def pair_terms(target, source, keep_mask):
    gap_time = target[0][:, None] - source[0][None, :]
    gap_time = jnp.where(keep_mask, gap_time, 0.0)
    row_gap = target[1][:, None] - source[1][None, :]
    col_gap = target[2][:, None] - source[2][None, :]
    squared = (row_gap * row_gap + col_gap * col_gap) * (cell_km * cell_km)
    contrib = source[3][None, :] * jnp.exp(-omori_power * jnp.log(gap_time + omori_offset) - squared * source[4][None, :])
    return jnp.sum(jnp.where(keep_mask, contrib, 0.0), axis=1)


def smooth_weights():
    offsets = jnp.arange(-rim_width, rim_width + 1).astype(jnp.float32)
    weights = jnp.exp(-offsets * offsets / (2.0 * smooth_sigma * smooth_sigma))
    return weights / jnp.sum(weights)


def column_pass(values, weights):
    length = values.shape[1]
    padded = jnp.pad(values, ((0, 0), (rim_width, rim_width)))
    summed = weights[0] * padded[:, 0:length]
    for offset in range(1, 2 * rim_width + 1):
        summed = summed + weights[offset] * padded[:, offset:offset + length]
    return summed


def row_pass(values, weights, length):
    summed = weights[0] * values[0:length]
    for offset in range(1, 2 * rim_width + 1):
        summed = summed + weights[offset] * values[offset:offset + length]
    return summed


def reference(times, cell_row, cell_col, magnitude, base_rate, productivity, spread):
    event_records = event_terms(times, cell_row, cell_col, magnitude, productivity, spread)
    block_count = EVENT_TOTAL // BLOCK_EVENTS
    padded = jnp.concatenate([jnp.zeros((5, NB * BLOCK_EVENTS), jnp.float32), event_records], axis=1)
    position = jnp.arange(BLOCK_EVENTS, dtype=jnp.int32)
    causal = position[None, :] < position[:, None]

    def one_block(block):
        own_block = lax.dynamic_slice_in_dim(event_records, (block * BLOCK_EVENTS).astype(jnp.int32), BLOCK_EVENTS, 1)
        earlier = lax.dynamic_slice_in_dim(padded, (block * BLOCK_EVENTS).astype(jnp.int32), NB * BLOCK_EVENTS, 1)
        return pair_terms(own_block, earlier, True) + pair_terms(own_block, own_block, causal)

    trigger = lax.map(one_block, jnp.arange(block_count, dtype=jnp.int32)).reshape(-1)
    intensity = base_rate + trigger
    log_event_intensity = jnp.log(intensity)
    share = (base_rate / intensity).astype(jnp.bfloat16)
    raw_grid = jnp.zeros((ROWS, COLS), jnp.float32).at[cell_row, cell_col].add(share.astype(jnp.float32))
    weights = smooth_weights()
    across = column_pass(raw_grid, weights)
    extended = jnp.pad(across, ((rim_width, rim_width), (0, 0)))
    density = row_pass(extended, weights, ROWS)
    return log_event_intensity, density
```

```python
import functools
import math

import jax
import jax.numpy as jnp
from jax import lax
from jax.experimental import pallas as pl
from jax.experimental.pallas import tpu as pltpu
from jax.sharding import PartitionSpec as P

NB = 2
LATITUDE_SPAN = 4
COLS = 16384

omori_power = 1.2
omori_offset = 0.5
cell_km = 0.1
smooth_sigma = 1.5
rim_width = 3

AXES = ("tm", "grid")
CHUNK = 32
LOG2E = math.log2(math.e)
WEIGHTS = [math.exp(-(b * b) / (2.0 * smooth_sigma**2)) for b in range(-rim_width, rim_width + 1)]
WEIGHT_SUM = sum(WEIGHTS)


def kernel(g_ref, prod_ref, spread_ref, logint_ref, dens_ref,
           t_s, r_s, c_s, l_s, v_s, b_s, pos_s, posm_s, cnt_v, cnt_s, a_buf, b_buf, x_s, sem):
    blocks = g_ref.shape[0]
    events = g_ref.shape[1] // 5
    nbin = prod_ref.shape[0]
    lo_cols = b_buf.shape[1]
    m_rows = a_buf.shape[1]
    batch = a_buf.shape[0]
    per_batch = batch // CHUNK
    own = lax.axis_index("tm") * lax.axis_size("grid") + lax.axis_index("grid")
    first_row = (own * LATITUDE_SPAN).astype(jnp.float32)

    times = g_ref[:, 0:events]
    rows = g_ref[:, events : 2 * events]
    mag = g_ref[:, 3 * events : 4 * events]
    t_s[0:blocks] = times
    r_s[0:blocks] = rows
    c_s[0:blocks] = g_ref[:, 2 * events : 3 * events]
    b_s[...] = g_ref[:, 4 * events : 5 * events]
    producing = jnp.full_like(mag, prod_ref[0])
    sigma = jnp.full_like(mag, spread_ref[0])
    for k in range(1, nbin):
        hit = mag == float(k)
        producing = jnp.where(hit, prod_ref[k], producing)
        sigma = jnp.where(hit, spread_ref[k], sigma)
    norm = (omori_power - 1.0) * omori_offset ** (omori_power - 1.0) / (2.0 * math.pi)
    area = sigma * sigma
    l_s[0:blocks] = jnp.log(producing * norm / area) * LOG2E
    v_s[0:blocks] = (0.5 * cell_km * cell_km * LOG2E) / area
    pad = (8, events)
    t_s[blocks : blocks + 8] = jnp.broadcast_to(times[0:1, 0:1], pad)
    r_s[blocks : blocks + 8] = jnp.zeros(pad, jnp.float32)
    c_s[blocks : blocks + 8] = jnp.zeros(pad, jnp.float32)
    l_s[blocks : blocks + 8] = jnp.full(pad, -1e30, jnp.float32)
    v_s[blocks : blocks + 8] = jnp.zeros(pad, jnp.float32)

    need = (rows >= first_row - rim_width) & (rows <= first_row + (LATITUDE_SPAN - 1 + rim_width))
    need_b = jnp.where(need, 1.0, 0.0).astype(jnp.bfloat16)
    upper = (
        lax.broadcasted_iota(jnp.int32, (events, events), 0)
        <= lax.broadcasted_iota(jnp.int32, (events, events), 1)
    )
    upper = jnp.where(upper, 1.0, 0.0).astype(jnp.bfloat16)
    pos = jnp.dot(need_b, upper, preferred_element_type=jnp.float32)
    pos_s[0:blocks] = pos
    posm_s[0:blocks] = jnp.where(need, pos, 0.0)
    ident = lax.broadcasted_iota(jnp.int32, pad, 1).astype(jnp.float32) + 1.0
    pos_s[blocks : blocks + 8] = ident
    posm_s[blocks : blocks + 8] = ident
    counts = lax.dot_general(
        jnp.ones((8, events), jnp.bfloat16), need_b, (((1,), (1,)), ((), ())),
        preferred_element_type=jnp.float32,
    )
    cnt_v[...] = counts.astype(jnp.int32)
    copy = pltpu.make_async_copy(cnt_v, cnt_s, sem)
    copy.start()

    rank = lax.broadcasted_iota(jnp.int32, (CHUNK, events), 0).astype(jnp.float32) + 1.0

    def row_of(ref, b):
        return ref[pl.ds(b, 1), :]

    def triggers(b, prow, first):
        order = rank + first
        pick = row_of(posm_s, prow) == order

        def taken(ref):
            return jnp.sum(jnp.where(pick, row_of(ref, b), 0.0), axis=1, keepdims=True)

        t_i, r_i, c_i, b_i = taken(t_s), taken(r_s), taken(c_s), taken(b_s)
        total = None
        for back in range(NB + 1):
            s = b if back == 0 else jnp.where(b >= back, b - back, blocks)
            gap = (t_i - row_of(t_s, s)) + omori_offset
            dr = r_i - row_of(r_s, s)
            dc = c_i - row_of(c_s, s)
            expo = (row_of(l_s, s) - (omori_power * LOG2E) * jnp.log(gap)) - (
                dr * dr + dc * dc
            ) * row_of(v_s, s)
            term = jnp.exp2(expo)
            if back == 0:
                term = jnp.where(row_of(pos_s, prow) < order, term, 0.0)
            total = term if total is None else total + term
        return pick, r_i, c_i, b_i, jnp.sum(total, axis=1, keepdims=True)

    lane_m = lax.broadcasted_iota(jnp.int32, (CHUNK, m_rows), 1)
    m_row = (lane_m % LATITUDE_SPAN).astype(jnp.float32)
    m_hi = (lane_m // LATITUDE_SPAN).astype(jnp.float32)
    lane_l = lax.broadcasted_iota(jnp.int32, (CHUNK, lo_cols), 1).astype(jnp.float32)

    def deposit(b, first, slot):
        _, r_i, c_i, b_i, trig = triggers(b, b, first)
        share = jnp.where(b_i > 0.0, b_i / (b_i + trig), 0.0)
        share = share.astype(jnp.bfloat16).astype(jnp.float32)
        hi = jnp.floor(c_i * (1.0 / lo_cols))
        lo = c_i - hi * lo_cols
        d = m_row - (r_i - first_row)
        d2 = d * d
        w = jnp.exp2(d2 * (-LOG2E / (2.0 * smooth_sigma**2))) * (share * (1.0 / WEIGHT_SUM))
        a = jnp.where((m_hi == hi) & (d2 < (rim_width + 0.5) ** 2), w, 0.0)
        a_buf[pl.ds(slot, CHUNK), :] = a.astype(jnp.bfloat16)
        b_buf[pl.ds(slot, CHUNK), :] = jnp.where(lane_l == lo, 1.0, 0.0).astype(jnp.bfloat16)

    def flush():
        x_s[8 : 8 + m_rows] += lax.dot_general(
            a_buf[...], b_buf[...], (((0,), (0,)), ((), ())), preferred_element_type=jnp.float32
        )

    x_s[...] = jnp.zeros_like(x_s)

    def batch_step(i, carry):
        for j in range(per_batch):
            deposit(i * per_batch + j, 0.0, j * CHUNK)
        flush()
        return carry

    lax.fori_loop(0, blocks // per_batch, batch_step, 0)

    out_row = jnp.zeros((1, events), jnp.float32)
    for k in range(events // CHUNK):
        pick, _, _, _, trig = triggers(own, blocks, float(k * CHUNK))
        out_row = out_row + jnp.sum(jnp.where(pick, trig, 0.0), axis=0, keepdims=True)
    logint_ref[...] = jnp.log(row_of(b_s, own) + out_row)

    copy.wait()
    a_buf[...] = jnp.zeros_like(a_buf)

    def extra_block(b, slot):
        def extra(c, slot):
            deposit(b, (c * CHUNK).astype(jnp.float32), pl.multiple_of(slot, CHUNK))
            slot = slot + CHUNK

            @pl.when(slot == batch)
            def _():
                flush()
                a_buf[...] = jnp.zeros_like(a_buf)

            return jnp.where(slot == batch, 0, slot)

        return lax.fori_loop(1, (cnt_s[0, b] + (CHUNK - 1)) // CHUNK, extra, slot)

    left = lax.fori_loop(0, blocks, extra_block, 0)

    @pl.when(left > 0)
    def _():
        flush()

    span = LATITUDE_SPAN
    mid = x_s[8 : 8 + m_rows]
    before = x_s[8 - span : 8 - span + m_rows]
    after = x_s[8 + span : 8 + span + m_rows]
    lane = lax.broadcasted_iota(jnp.int32, (m_rows, lo_cols), 1)
    acc = mid * (WEIGHTS[rim_width] / WEIGHT_SUM)
    for b in range(1, rim_width + 1):
        from_left = jnp.where(lane < b, pltpu.roll(before, b, 1), pltpu.roll(mid, b, 1))
        from_right = jnp.where(
            lane >= lo_cols - b, pltpu.roll(after, lo_cols - b, 1), pltpu.roll(mid, lo_cols - b, 1)
        )
        acc = acc + (from_left + from_right) * (WEIGHTS[rim_width + b] / WEIGHT_SUM)
    for h in range(m_rows // span):
        dens_ref[:, h * lo_cols : (h + 1) * lo_cols] = acc[h * span : (h + 1) * span]


def body(times, cell_row, cell_col, magnitude, base_rate, productivity, spread):
    events = times.shape[0]
    count = lax.axis_size(AXES)
    f32 = jnp.float32
    payload = jnp.concatenate(
        [times, cell_row.astype(f32), cell_col.astype(f32), magnitude.astype(f32), base_rate]
    )
    gathered = lax.all_to_all(
        jnp.broadcast_to(payload[None], (count, payload.shape[0])), AXES, 0, 0, tiled=True
    )
    lo_cols = 256
    m_rows = LATITUDE_SPAN * (COLS // lo_cols)
    per_batch = math.gcd(count, 8)
    field = pltpu.VMEM((count + 8, events), f32)
    log_intensity, density = pl.pallas_call(
        kernel,
        out_shape=(
            jax.ShapeDtypeStruct((1, events), f32),
            jax.ShapeDtypeStruct((LATITUDE_SPAN, COLS), f32),
        ),
        in_specs=[
            pl.BlockSpec(memory_space=pltpu.VMEM),
            pl.BlockSpec(memory_space=pltpu.SMEM),
            pl.BlockSpec(memory_space=pltpu.SMEM),
        ],
        out_specs=(
            pl.BlockSpec(memory_space=pltpu.VMEM),
            pl.BlockSpec(memory_space=pltpu.VMEM),
        ),
        scratch_shapes=[
            field, field, field, field, field,
            pltpu.VMEM((count, events), f32),
            field, field,
            pltpu.VMEM((8, count), jnp.int32),
            pltpu.SMEM((8, count), jnp.int32),
            pltpu.VMEM((per_batch * CHUNK, m_rows), jnp.bfloat16),
            pltpu.VMEM((per_batch * CHUNK, lo_cols), jnp.bfloat16),
            pltpu.VMEM((m_rows + 16, lo_cols), f32),
            pltpu.SemaphoreType.DMA,
        ],
    )(gathered, productivity, spread)
    return (log_intensity.reshape(events), density)


def solution(mesh):
    in_specs = (P(AXES), P(AXES), P(AXES), P(AXES), P(AXES), P(), P())
    out_specs = (P(AXES), P(AXES, None))
    return jax.shard_map(body, mesh=mesh, in_specs=in_specs, out_specs=out_specs, check_vma=False)
```

```python
import math

import jax
import jax.numpy as jnp
from jax import lax
from jax.experimental import pallas as pl
from jax.experimental.pallas import tpu as pltpu
from jax.sharding import PartitionSpec as P

NB = 2
LATITUDE_SPAN = 4
COLS = 16384

omori_power = 1.2
omori_offset = 0.5
cell_km = 0.1
smooth_sigma = 1.5
rim_width = 3

AXES = ("tm", "grid")
LANES = 128
UNIT = 8
STEP = 8
BATCH = 256
LO_COLS = 256
M_ROWS = LATITUDE_SPAN * (COLS // LO_COLS)
LOG2E = math.log2(math.e)
WEIGHTS = [math.exp(-(b * b) / (2.0 * smooth_sigma**2)) for b in range(-rim_width, rim_width + 1)]
WEIGHT_SUM = sum(WEIGHTS)
MIB = 1 << 20


def spread_kernel(t_ref, r_ref, c_ref, m_ref, b_ref, out_ref):
    events = t_ref.shape[1]
    shape = (out_ref.shape[0], 1, events)
    for k, ref in enumerate([t_ref, r_ref, c_ref, m_ref, b_ref]):
        row = ref[...].astype(jnp.float32)
        out_ref[:, :, k * events : (k + 1) * events] = jnp.broadcast_to(row[None], shape)


def kernel(g_ref, prod_ref, spread_ref, logint_ref, dens_ref,
           t_s, r_s, c_s, l_s, v_s, b_s, pos_s, posm_s,
           blk_v, fst_v, blk_s, fst_s, sel_s, dep_s, a_buf, b_buf, x_s, sems):
    f32 = jnp.float32
    bf16 = jnp.bfloat16
    blocks = g_ref.shape[0]
    events = g_ref.shape[2] // 5
    halves = events // LANES
    nbin = prod_ref.shape[0]
    listed = blk_v.shape[1]
    own = lax.axis_index("tm") * lax.axis_size("grid") + lax.axis_index("grid")
    first_row = (own * LATITUDE_SPAN).astype(f32)

    times = g_ref[:, 0, 0:events]
    rows = g_ref[:, 0, events : 2 * events]
    mag = g_ref[:, 0, 3 * events : 4 * events]

    need = (rows >= first_row - rim_width) & (rows <= first_row + (LATITUDE_SPAN - 1 + rim_width))
    need_f = jnp.where(need, 1.0, 0.0)
    upper = (
        lax.broadcasted_iota(jnp.int32, (events, events), 0)
        <= lax.broadcasted_iota(jnp.int32, (events, events), 1)
    )
    upper = jnp.where(upper, 1.0, 0.0).astype(bf16)
    pos = jnp.dot(need_f.astype(bf16), upper, preferred_element_type=f32)
    pos_s[0:blocks] = pos
    posm_s[0:blocks] = jnp.where(need, pos, 0.0)
    pad = (8, events)
    pos_s[blocks : blocks + 8] = jnp.zeros(pad, f32)
    posm_s[blocks : blocks + 8] = jnp.zeros(pad, f32)

    count = jnp.sum(need_f, axis=1, keepdims=True)
    units = jnp.floor((count + (UNIT - 1)) * (1.0 / UNIT))
    lower = (
        lax.broadcasted_iota(jnp.int32, (blocks, blocks), 0)
        >= lax.broadcasted_iota(jnp.int32, (blocks, blocks), 1)
    )
    ends = jnp.dot(
        jnp.where(lower, 1.0, 0.0).astype(bf16),
        jnp.broadcast_to(units, (blocks, LANES)).astype(bf16),
        preferred_element_type=f32,
    )
    lane = lax.broadcasted_iota(jnp.int32, (1, LANES), 1)

    def list_part(k, carry):
        at = k * LANES
        if not isinstance(k, int):
            at = pl.multiple_of(at, LANES)
        u = (lane + at).astype(f32)
        done = ends <= u
        blk_v[:, pl.ds(at, LANES)] = jnp.sum(
            jnp.where(done, 1.0, 0.0), axis=0, keepdims=True
        ).astype(jnp.int32)
        start = jnp.max(jnp.where(done, ends, 0.0), axis=0, keepdims=True)
        fst_v[:, pl.ds(at, LANES)] = (u - start) * float(UNIT)
        return carry

    if listed <= 16 * LANES:
        for k in range(listed // LANES):
            list_part(k, 0)
    else:
        lax.fori_loop(0, listed // LANES, list_part, 0)
    copies = [
        pltpu.make_async_copy(blk_v, blk_s, sems.at[0]),
        pltpu.make_async_copy(fst_v, fst_s, sems.at[1]),
    ]
    for copy in copies:
        copy.start()

    t_s[0:blocks] = times
    r_s[0:blocks] = rows
    c_s[0:blocks] = g_ref[:, 0, 2 * events : 3 * events]
    b_s[0:blocks] = g_ref[:, 0, 4 * events : 5 * events]
    producing = jnp.full_like(mag, prod_ref[0])
    sigma = jnp.full_like(mag, spread_ref[0])
    for k in range(1, nbin):
        hit = mag == float(k)
        producing = jnp.where(hit, prod_ref[k], producing)
        sigma = jnp.where(hit, spread_ref[k], sigma)
    norm = (omori_power - 1.0) * omori_offset ** (omori_power - 1.0) / (2.0 * math.pi)
    area = sigma * sigma
    l_s[0:blocks] = jnp.log(producing * norm / area) * LOG2E
    v_s[0:blocks] = (0.5 * cell_km * cell_km * LOG2E) / area
    t_s[blocks : blocks + 8] = jnp.broadcast_to(times[0:1, 0:1], pad)
    r_s[blocks : blocks + 8] = jnp.zeros(pad, f32)
    c_s[blocks : blocks + 8] = jnp.zeros(pad, f32)
    b_s[blocks : blocks + 8] = jnp.zeros(pad, f32)
    l_s[blocks : blocks + 8] = jnp.full(pad, -1e30, f32)
    v_s[blocks : blocks + 8] = jnp.zeros(pad, f32)
    x_s[...] = jnp.zeros_like(x_s)
    sel_s[...] = jnp.zeros_like(sel_s)
    dep_s[...] = jnp.zeros_like(dep_s)

    def part(ref, b, h):
        return ref[pl.ds(b, 1), :][:, h * LANES : (h + 1) * LANES]

    def source(b, back):
        return b if back == 0 else jnp.where(b >= back, b - back, blocks)

    def lane_sums(t_i, r_i, c_i, b, before):
        total = None
        for back in range(NB + 1):
            s = source(b, back)
            for h in range(halves):
                gap = (t_i - part(t_s, s, h)) + omori_offset
                dr = r_i - part(r_s, s, h)
                dc = c_i - part(c_s, s, h)
                expo = (part(l_s, s, h) - (omori_power * LOG2E) * jnp.log(gap)) - (
                    dr * dr + dc * dc
                ) * part(v_s, s, h)
                term = jnp.exp2(expo)
                if back == 0:
                    term = jnp.where(before(h), term, 0.0)
                total = term if total is None else total + term
        return jnp.sum(total, axis=1, keepdims=True)

    sub = lax.broadcasted_iota(jnp.int32, (UNIT, LANES), 0)
    lane_u = lax.broadcasted_iota(jnp.int32, (UNIT, LANES), 1)
    own_rows = jnp.concatenate(
        [t_s[pl.ds(own, 1), :], r_s[pl.ds(own, 1), :], c_s[pl.ds(own, 1), :], jnp.zeros((5, events), f32)]
    )
    own_cols = jnp.transpose(own_rows)
    for h in range(halves):
        found = jnp.zeros((UNIT, LANES), f32)
        for j in range(LANES // UNIT):
            at = h * LANES + j * UNIT
            cols = own_cols[at : at + UNIT]
            target = sub + j * UNIT

            def before(k, h=h, target=target):
                return lane_u + (k - h) * LANES < target

            trig = lane_sums(cols[:, 0:1], cols[:, 1:2], cols[:, 2:3], own, before)
            found = found + jnp.where(lane_u == target, trig, 0.0)
        found = jnp.sum(found, axis=0, keepdims=True)
        logint_ref[:, h * LANES : (h + 1) * LANES] = jnp.log(part(b_s, own, h) + found)

    for copy in copies:
        copy.wait()
    total_units = (listed - 1) - (fst_s[0, listed - 1] * (1.0 / UNIT)).astype(jnp.int32)

    rank = sub.astype(f32) + 1.0
    slots = STEP * UNIT
    m_row = (lax.broadcasted_iota(jnp.int32, (slots, LANES), 1) % LATITUDE_SPAN).astype(f32)
    lane_s = lax.broadcasted_iota(jnp.int32, (slots, LANES), 1)
    m_hi = (lane_s // LATITUDE_SPAN).astype(f32)
    lane_f = lane_s.astype(f32)

    def flush():
        x_s[8 : 8 + M_ROWS] += lax.dot_general(
            a_buf[...], b_buf[...], (((0,), (0,)), ((), ())), preferred_element_type=f32
        )

    def step(i, carry):
        r_i, c_i, b_i, trig = dep_s[0], dep_s[1], dep_s[2], dep_s[3]
        share = jnp.where(b_i > 0.0, b_i / (b_i + trig), 0.0)
        share = share.astype(bf16).astype(f32)
        hi = jnp.floor(c_i * (1.0 / LO_COLS))
        lo = c_i - hi * LO_COLS
        d = m_row - (r_i - first_row)
        d2 = d * d
        w = jnp.exp2(d2 * (-LOG2E / (2.0 * smooth_sigma**2))) * (share * (1.0 / WEIGHT_SUM))
        w = jnp.where(d2 < (rim_width + 0.5) ** 2, w, 0.0)
        slot = pl.multiple_of(lax.rem(i + (BATCH // slots - 2), BATCH // slots) * slots, slots)
        for h in range(M_ROWS // LANES):
            a = jnp.where(m_hi == hi - float(h * (LANES // LATITUDE_SPAN)), w, 0.0)
            a_buf[pl.ds(slot, slots), h * LANES : (h + 1) * LANES] = a.astype(bf16)
        for h in range(LO_COLS // LANES):
            b = jnp.where(lane_f == lo - float(h * LANES), 1.0, 0.0)
            b_buf[pl.ds(slot, slots), h * LANES : (h + 1) * LANES] = b.astype(bf16)
        for j in range(STEP):
            u = jnp.maximum((i - 1) * STEP + j, 0)
            b = blk_s[0, u]
            order = rank + fst_s[0, u]
            at = slice(j * UNIT, (j + 1) * UNIT)
            t_i, r_i, c_i = sel_s[0, at], sel_s[1, at], sel_s[2, at]
            trig = lane_sums(t_i, r_i, c_i, b, lambda h: part(pos_s, b, h) < order)
            dep_s[0, at] = r_i
            dep_s[1, at] = c_i
            dep_s[2, at] = sel_s[3, at]
            dep_s[3, at] = jnp.broadcast_to(trig, (UNIT, LANES))
        for j in range(STEP):
            u = i * STEP + j
            b = blk_s[0, u]
            order = rank + fst_s[0, u]
            picks = [part(posm_s, b, h) == order for h in range(halves)]
            for k, ref in enumerate((t_s, r_s, c_s, b_s)):
                value = None
                for h in range(halves):
                    piece = jnp.where(picks[h], part(ref, b, h), 0.0)
                    value = piece if value is None else value + piece
                value = jnp.sum(value, axis=1, keepdims=True)
                sel_s[k, j * UNIT : (j + 1) * UNIT] = jnp.broadcast_to(value, (UNIT, LANES))

        @pl.when(slot == BATCH - slots)
        def _():
            flush()
            a_buf[...] = jnp.zeros_like(a_buf)

        return carry

    a_buf[...] = jnp.zeros_like(a_buf)
    b_buf[...] = jnp.zeros_like(b_buf)
    lax.fori_loop(0, (total_units + (STEP - 1)) // STEP + 2, step, 0)
    flush()

    span = LATITUDE_SPAN
    wide = LO_COLS // LANES
    tall = 16
    lane_t = lax.broadcasted_iota(jnp.int32, (tall, LANES), 1)
    for m in range(0, M_ROWS, tall):
        def tile(shift, h):
            return x_s[8 + m + shift : 8 + m + shift + tall, h * LANES : (h + 1) * LANES]

        mids = [tile(0, h) for h in range(wide)]
        lefts = [tile(-span, wide - 1)] + mids[:-1]
        rights = mids[1:] + [tile(span, 0)]
        for h in range(wide):
            acc = mids[h] * (WEIGHTS[rim_width] / WEIGHT_SUM)
            for b in range(1, rim_width + 1):
                from_left = pltpu.roll(jnp.where(lane_t >= LANES - b, lefts[h], mids[h]), b, 1)
                from_right = pltpu.roll(jnp.where(lane_t < b, rights[h], mids[h]), LANES - b, 1)
                acc = acc + (from_left + from_right) * (WEIGHTS[rim_width + b] / WEIGHT_SUM)
            for q in range(tall // span):
                at = (m // span + q) * LO_COLS + h * LANES
                dens_ref[:, at : at + LANES] = acc[q * span : (q + 1) * span]


def body(times, cell_row, cell_col, magnitude, base_rate, productivity, spread):
    events = times.shape[0]
    blocks = lax.axis_size(AXES)
    f32 = jnp.float32
    rows = [x.reshape(1, events) for x in (times, cell_row, cell_col, magnitude, base_rate)]
    vmem = pl.BlockSpec(memory_space=pltpu.VMEM)
    smem = pl.BlockSpec(memory_space=pltpu.SMEM)
    spread_out = pl.pallas_call(
        spread_kernel,
        out_shape=jax.ShapeDtypeStruct((blocks, 1, 5 * events), f32),
        in_specs=[vmem] * 5,
        out_specs=vmem,
        compiler_params=pltpu.CompilerParams(vmem_limit_bytes=16 * MIB),
    )(*rows)
    gathered = lax.all_to_all(spread_out, AXES, 0, 0, tiled=True)
    listed = blocks * events // UNIT + LANES
    field = pltpu.VMEM((blocks + 8, events), f32)
    log_intensity, density = pl.pallas_call(
        kernel,
        out_shape=(
            jax.ShapeDtypeStruct((1, events), f32),
            jax.ShapeDtypeStruct((LATITUDE_SPAN, COLS), f32),
        ),
        in_specs=[vmem, smem, smem],
        out_specs=(vmem, vmem),
        scratch_shapes=[field] * 8
        + [
            pltpu.VMEM((1, listed), jnp.int32),
            pltpu.VMEM((1, listed), f32),
            pltpu.SMEM((1, listed), jnp.int32),
            pltpu.SMEM((1, listed), f32),
            pltpu.VMEM((4, STEP * UNIT, LANES), f32),
            pltpu.VMEM((4, STEP * UNIT, LANES), f32),
            pltpu.VMEM((BATCH, M_ROWS), jnp.bfloat16),
            pltpu.VMEM((BATCH, LO_COLS), jnp.bfloat16),
            pltpu.VMEM((M_ROWS + 16, LO_COLS), f32),
            pltpu.SemaphoreType.DMA((2,)),
        ],
        compiler_params=pltpu.CompilerParams(vmem_limit_bytes=32 * MIB),
    )(gathered, productivity, spread)
    return (log_intensity.reshape(events), density)


def solution(mesh):
    in_specs = (P(AXES), P(AXES), P(AXES), P(AXES), P(AXES), P(), P())
    out_specs = (P(AXES), P(AXES, None))
    return jax.shard_map(body, mesh=mesh, in_specs=in_specs, out_specs=out_specs, check_vma=False)
```

```python
import math

import jax
import jax.numpy as jnp
from jax import lax
from jax.experimental import pallas as pl
from jax.experimental.pallas import tpu as pltpu
from jax.sharding import PartitionSpec as P

NB = 2
LATITUDE_SPAN = 4
COLS = 16384

omori_power = 1.2
omori_offset = 0.5
cell_km = 0.1
smooth_sigma = 1.5
rim_width = 3

AXES = ("tm", "grid")
LANES = 128
UNIT = 8
STEP = 8
BATCH = 256
LO_COLS = 256
M_ROWS = LATITUDE_SPAN * (COLS // LO_COLS)
LOG2E = math.log2(math.e)
WEIGHTS = [math.exp(-(b * b) / (2.0 * smooth_sigma**2)) for b in range(-rim_width, rim_width + 1)]
WEIGHT_SUM = sum(WEIGHTS)
MIB = 1 << 20
FT = jnp.bfloat16


def spread_kernel(t_ref, r_ref, c_ref, m_ref, b_ref, prod_ref, spread_ref, out_ref, l_ref, v_ref):
    norm = (omori_power - 1.0) * omori_offset ** (omori_power - 1.0) / (2.0 * math.pi)
    area = spread_ref[...] * spread_ref[...]
    l_ref[...] = jnp.log(prod_ref[...] * norm / area) * LOG2E
    v_ref[...] = (0.5 * cell_km * cell_km * LOG2E) / area
    events = t_ref.shape[1]
    shape = (out_ref.shape[0], 1, events)
    for k, ref in enumerate([t_ref, r_ref, c_ref, m_ref, b_ref]):
        row = ref[...].astype(jnp.float32)
        out_ref[:, :, k * events : (k + 1) * events] = jnp.broadcast_to(row[None], shape)


def kernel(g_ref, lof_ref, vof_ref, logint_ref, dens_ref,
           t_s, l_s, v_s, pos_s, posm_s, own_s,
           blk_v, fst_v, blk_s, fst_s, sel_s, dep_s, a_buf, b_buf, x_s, sems):
    f32 = jnp.float32
    bf16 = jnp.bfloat16
    i32 = jnp.int32
    blocks = g_ref.shape[0]
    events = g_ref.shape[2] // 5
    halves = events // LANES
    nbin = lof_ref.shape[1]
    listed = blk_v.shape[1]
    tall = 8
    own = lax.axis_index("tm") * lax.axis_size("grid") + lax.axis_index("grid")
    first_row = (own * LATITUDE_SPAN).astype(f32)

    l_of = lof_ref[...]
    v_of = vof_ref[...]

    def fields(k, carry):
        at = pl.ds(pl.multiple_of(k * tall, tall), tall)
        t_s[at] = g_ref[at, 0, 0:events]
        rows = g_ref[at, 0, events : 2 * events]
        mag = g_ref[at, 0, 3 * events : 4 * events]
        need = (rows >= first_row - rim_width) & (
            rows <= first_row + (LATITUDE_SPAN - 1 + rim_width)
        )
        posm_s[at] = jnp.where(need, 1.0, 0.0)
        l_j = jnp.broadcast_to(l_of[:, 0:1], mag.shape)
        v_j = jnp.broadcast_to(v_of[:, 0:1], mag.shape)
        for n in range(1, nbin):
            hit = mag == float(n)
            l_j = jnp.where(hit, l_of[:, n : n + 1], l_j)
            v_j = jnp.where(hit, v_of[:, n : n + 1], v_j)
        l_s[at] = l_j
        v_s[at] = v_j
        return carry

    lax.fori_loop(0, blocks // tall, fields, 0)
    pad = (tall, events)
    t_s[blocks : blocks + tall] = jnp.broadcast_to(g_ref[0:1, 0, 0:1], pad)
    l_s[blocks : blocks + tall] = jnp.full(pad, -1e30, f32)

    need_f = posm_s[...]
    upper = lax.broadcasted_iota(i32, (events, events), 0) <= lax.broadcasted_iota(
        i32, (events, events), 1
    )
    upper = jnp.where(upper, 1.0, 0.0).astype(bf16)
    pos = jnp.dot(need_f.astype(bf16), upper, preferred_element_type=f32)
    pos_s[...] = pos
    posm_s[...] = need_f * pos

    count = jnp.sum(need_f, axis=1, keepdims=True)
    units = jnp.floor((count + (UNIT - 1)) * (1.0 / UNIT))
    lower = lax.broadcasted_iota(i32, (blocks, blocks), 0) >= lax.broadcasted_iota(
        i32, (blocks, blocks), 1
    )
    ends = jnp.dot(
        jnp.where(lower, 1.0, 0.0).astype(bf16),
        jnp.broadcast_to(units, (blocks, LANES)).astype(bf16),
        preferred_element_type=f32,
    )
    lane = lax.broadcasted_iota(i32, (1, LANES), 1)
    beyond = 1e6

    def list_part(k, carry):
        at = k * LANES
        if not isinstance(k, int):
            at = pl.multiple_of(at, LANES)
        u = (lane + at).astype(f32)
        done = ends <= u
        blk = jnp.sum(jnp.where(done, 1.0, 0.0), axis=0, keepdims=True)
        start = jnp.max(jnp.where(done, ends, 0.0), axis=0, keepdims=True)
        last = float(blocks - 1)
        blk_v[:, pl.ds(at, LANES)] = jnp.minimum(blk, last).astype(i32)
        fst_v[:, pl.ds(at, LANES)] = (u - start) * float(UNIT) + jnp.where(blk > last, beyond, 0.0)
        return carry

    if listed <= 16 * LANES:
        for k in range(listed // LANES):
            list_part(k, 0)
    else:
        lax.fori_loop(0, listed // LANES, list_part, 0)
    copies = [
        pltpu.make_async_copy(blk_v, blk_s, sems.at[0]),
        pltpu.make_async_copy(fst_v, fst_s, sems.at[1]),
    ]
    for copy in copies:
        copy.start()

    x_s[...] = jnp.zeros_like(x_s)
    dep_s[...] = jnp.zeros_like(dep_s)
    a_buf[...] = jnp.zeros_like(a_buf)
    b_buf[...] = jnp.zeros_like(b_buf)

    def part(ref, b, h):
        return ref[pl.ds(b, 1), :][:, h * LANES : (h + 1) * LANES]

    def given(field, b, h):
        at = field * events + h * LANES
        return g_ref[b, 0:1, at : at + LANES]

    def lane_sums(t_i, r_i, c_i, b, before):
        total = None
        for back in range(NB + 1):
            near = b if back == 0 else jnp.maximum(b - back, 0)
            s = b if back == 0 else jnp.where(b >= back, b - back, blocks)
            for h in range(halves):
                gap = (t_i - part(t_s, s, h)) + omori_offset
                dr = r_i - given(1, near, h)
                dc = c_i - given(2, near, h)
                expo = (part(l_s, s, h) - (omori_power * LOG2E) * jnp.log(gap)) - (
                    dr * dr + dc * dc
                ) * part(v_s, near, h)
                term = jnp.exp2(expo)
                if back == 0:
                    term = jnp.where(before(h), term, 0.0)
                total = term if total is None else total + term
        return jnp.sum(total, axis=1, keepdims=True)

    sub_f = lax.broadcasted_iota(i32, (UNIT, LANES), 0).astype(f32)
    lane_f = lax.broadcasted_iota(i32, (UNIT, LANES), 1).astype(f32)
    own_rows = jnp.concatenate(
        [g_ref[own, 0:1, k * events : (k + 1) * events] for k in range(3)]
        + [jnp.zeros((5, events), f32)]
    )
    own_cols = jnp.transpose(own_rows)
    for k in range(3):
        own_s[k] = jnp.broadcast_to(own_cols[:, k : k + 1], (events, LANES))

    def own_step(k, found):
        for j in range(STEP):
            at = k * (STEP * UNIT) + j * UNIT
            target = sub_f + at.astype(f32)
            t_i, r_i, c_i = (own_s[n, pl.ds(pl.multiple_of(at, UNIT), UNIT)] for n in range(3))
            trig = lane_sums(t_i, r_i, c_i, own, lambda h: lane_f + h * LANES < target)
            found = tuple(
                found[h] + jnp.where(lane_f + h * LANES == target, trig, 0.0) for h in range(halves)
            )
        return found

    found = lax.fori_loop(
        0, events // (STEP * UNIT), own_step, tuple(jnp.zeros((UNIT, LANES), f32) for _ in range(halves))
    )
    for h in range(halves):
        trig = jnp.sum(found[h], axis=0, keepdims=True)
        logint_ref[:, h * LANES : (h + 1) * LANES] = jnp.log(given(4, own, h) + trig)

    for copy in copies:
        copy.wait()
    total_units = (listed - 1) - ((fst_s[0, listed - 1] - beyond) * (1.0 / UNIT)).astype(i32)

    rank = sub_f + 1.0
    slots = STEP * UNIT
    steps = BATCH // slots
    lane_s = lax.broadcasted_iota(i32, (slots, LANES), 1)
    m_row = (lane_s % LATITUDE_SPAN).astype(f32)
    col_blocks = M_ROWS // LATITUDE_SPAN
    m_hi = []
    for h in range(M_ROWS // LANES):
        m = lane_s + h * LANES
        m_hi.append((m // LATITUDE_SPAN % 2 * (col_blocks // 2) + m // (2 * LATITUDE_SPAN)).astype(FT))
    l_lo = [(lane_s + h * LANES).astype(FT) for h in range(LO_COLS // LANES)]
    zero, one = jnp.zeros((), FT), jnp.ones((), FT)

    def flush(size):
        x_s[8 : 8 + M_ROWS] += lax.dot_general(
            a_buf[0:size], b_buf[0:size], (((0,), (0,)), ((), ())), preferred_element_type=f32
        )

    def factors(slot):
        r_i, c_i, b_i, trig = dep_s[0], dep_s[1], dep_s[2], dep_s[3]
        share = jnp.where(b_i > 0.0, b_i / (b_i + trig), 0.0)
        share = share.astype(bf16).astype(f32)
        hi = jnp.floor(c_i * (1.0 / LO_COLS))
        lo = (c_i - hi * LO_COLS).astype(FT)
        hi = hi.astype(FT)
        d = m_row - (r_i - first_row)
        d2 = d * d
        w = jnp.exp2(d2 * (-LOG2E / (2.0 * smooth_sigma**2))) * share
        w = jnp.where(d2 < (rim_width + 0.5) ** 2, w, 0.0).astype(FT)
        at = pl.ds(pl.multiple_of(slot * slots, slots), slots)
        for h in range(M_ROWS // LANES):
            a_buf[at, h * LANES : (h + 1) * LANES] = jnp.where(m_hi[h] == hi, w, zero).astype(bf16)
        for h in range(LO_COLS // LANES):
            b_buf[at, h * LANES : (h + 1) * LANES] = jnp.where(l_lo[h] == lo, one, zero).astype(bf16)

    def unit_triggers(i):
        for j in range(STEP):
            u = i * STEP + j
            b = blk_s[0, u]
            order = rank + fst_s[0, u]
            at = slice(j * UNIT, (j + 1) * UNIT)
            t_i, r_i, c_i = sel_s[0, at], sel_s[1, at], sel_s[2, at]
            trig = lane_sums(t_i, r_i, c_i, b, lambda h: part(pos_s, b, h) < order)
            dep_s[0, at] = r_i
            dep_s[1, at] = c_i
            dep_s[2, at] = sel_s[3, at]
            dep_s[3, at] = jnp.broadcast_to(trig, (UNIT, LANES))

    def pick_events(i):
        for j in range(STEP):
            u = i * STEP + j
            b = blk_s[0, u]
            order = rank + fst_s[0, u]
            picks = [part(posm_s, b, h) == order for h in range(halves)]
            for k, field in enumerate((0, 1, 2, 4)):
                value = None
                for h in range(halves):
                    piece = jnp.where(picks[h], given(field, b, h), 0.0)
                    value = piece if value is None else value + piece
                value = jnp.sum(value, axis=1, keepdims=True)
                sel_s[k, j * UNIT : (j + 1) * UNIT] = jnp.broadcast_to(value, (UNIT, LANES))

    total_steps = (total_units + (STEP - 1)) // STEP
    pick_events(0)

    def batch(q, carry):
        @pl.when(q > 0)
        def _():
            flush(BATCH)
            a_buf[...] = jnp.zeros_like(a_buf)

        def step(k, carry):
            i = q * steps + k
            factors(k)
            unit_triggers(i)
            pick_events(i + 1)
            return carry

        return lax.fori_loop(0, jnp.minimum(total_steps - q * steps, steps), step, 0)

    batches = (total_steps + (steps - 1)) // steps
    lax.fori_loop(0, batches, batch, 0)
    factors(total_steps - jnp.maximum(batches - 1, 0) * steps)
    flush(BATCH + slots)

    span = LATITUDE_SPAN
    wide = LO_COLS // LANES
    middle = (col_blocks // 2) * LO_COLS
    zeros = jnp.zeros((span, LO_COLS), f32)
    x_s[0:8] = jnp.concatenate([zeros, x_s[M_ROWS : M_ROWS + span]])
    x_s[8 + M_ROWS : 16 + M_ROWS] = jnp.concatenate([x_s[8 + span : 16], zeros])
    lane_t = lax.broadcasted_iota(i32, (8, LANES), 1)
    per = 4

    def columns(g, carry):
        for p in range(per):
            m = g * (8 * per) + 8 * p

            def tile(shift, h):
                return x_s[pl.ds(pl.multiple_of(m + 8 + shift, 8), 8), h * LANES : (h + 1) * LANES]

            mids = [tile(0, h) for h in range(wide)]
            lefts = [tile(-8, wide - 1)] + mids[:-1]
            rights = mids[1:] + [tile(8, 0)]
            for h in range(wide):
                acc = mids[h] * (WEIGHTS[rim_width] / WEIGHT_SUM**2)
                for b in range(1, rim_width + 1):
                    from_left = pltpu.roll(jnp.where(lane_t >= LANES - b, lefts[h], mids[h]), b, 1)
                    from_right = pltpu.roll(jnp.where(lane_t < b, rights[h], mids[h]), LANES - b, 1)
                    acc = acc + (from_left + from_right) * (WEIGHTS[rim_width + b] / WEIGHT_SUM**2)
                at = (g * per + p) * LO_COLS + h * LANES
                for half in range(2):
                    place = pl.ds(pl.multiple_of(at + half * middle, LANES), LANES)
                    dens_ref[:, place] = acc[half * span : (half + 1) * span]
        return carry

    lax.fori_loop(0, M_ROWS // (8 * per), columns, 0)


def body(times, cell_row, cell_col, magnitude, base_rate, productivity, spread):
    events = times.shape[0]
    blocks = lax.axis_size(AXES)
    f32 = jnp.float32
    rows = [x.reshape(1, events) for x in (times, cell_row, cell_col, magnitude, base_rate)]
    vmem = pl.BlockSpec(memory_space=pltpu.VMEM)
    rows += [x.reshape(1, -1) for x in (productivity, spread)]
    table = jax.ShapeDtypeStruct((1, productivity.shape[0]), f32)
    spread_out, l_table, v_table = pl.pallas_call(
        spread_kernel,
        out_shape=(jax.ShapeDtypeStruct((blocks, 1, 5 * events), f32), table, table),
        in_specs=[vmem] * 7,
        out_specs=(vmem, vmem, vmem),
        compiler_params=pltpu.CompilerParams(vmem_limit_bytes=16 * MIB),
    )(*rows)
    gathered = lax.all_to_all(spread_out, AXES, 0, 0, tiled=True)
    listed = blocks * events // UNIT + LANES
    padded = pltpu.VMEM((blocks + 8, events), f32)
    field = pltpu.VMEM((blocks, events), f32)
    log_intensity, density = pl.pallas_call(
        kernel,
        out_shape=(
            jax.ShapeDtypeStruct((1, events), f32),
            jax.ShapeDtypeStruct((LATITUDE_SPAN, COLS), f32),
        ),
        in_specs=[vmem, vmem, vmem],
        out_specs=(vmem, vmem),
        scratch_shapes=[
            padded, padded, field, field, field,
            pltpu.VMEM((3, events, LANES), f32),
            pltpu.VMEM((1, listed), jnp.int32),
            pltpu.VMEM((1, listed), f32),
            pltpu.SMEM((1, listed), jnp.int32),
            pltpu.SMEM((1, listed), f32),
            pltpu.VMEM((4, STEP * UNIT, LANES), f32),
            pltpu.VMEM((4, STEP * UNIT, LANES), f32),
            pltpu.VMEM((BATCH + STEP * UNIT, M_ROWS), jnp.bfloat16),
            pltpu.VMEM((BATCH + STEP * UNIT, LO_COLS), jnp.bfloat16),
            pltpu.VMEM((M_ROWS + 16, LO_COLS), f32),
            pltpu.SemaphoreType.DMA((2,)),
        ],
        compiler_params=pltpu.CompilerParams(vmem_limit_bytes=32 * MIB),
    )(gathered, l_table, v_table)
    return (log_intensity.reshape(events), density)


def solution(mesh):
    in_specs = (P(AXES), P(AXES), P(AXES), P(AXES), P(AXES), P(), P())
    out_specs = (P(AXES), P(AXES, None))
    return jax.shard_map(body, mesh=mesh, in_specs=in_specs, out_specs=out_specs, check_vma=False)
```

```python
import math

import jax
import jax.numpy as jnp
from jax import lax
from jax.experimental import pallas as pl
from jax.experimental.pallas import tpu as pltpu
from jax.sharding import PartitionSpec as P

NB = 2
LATITUDE_SPAN = 4
COLS = 16384

omori_power = 1.2
omori_offset = 0.5
cell_km = 0.1
smooth_sigma = 1.5
rim_width = 3

AXES = ("tm", "grid")
LANES = 128
UNIT = 8
STEP = 16
OWN_STEP = 16
BATCH = 512
LO_COLS = 256
M_ROWS = LATITUDE_SPAN * (COLS // LO_COLS)
LOG2E = math.log2(math.e)
WEIGHTS = [math.exp(-(b * b) / (2.0 * smooth_sigma**2)) for b in range(-rim_width, rim_width + 1)]
WEIGHT_SUM = sum(WEIGHTS)
MIB = 1 << 20
PER = 32
FIELDS = 8
T, R, C, L, V, B, RANK, PICK = range(FIELDS)
FT = jnp.bfloat16


def spread_kernel(t_ref, r_ref, c_ref, m_ref, b_ref, prod_ref, spread_ref, out_ref, l_ref, v_ref):
    norm = (omori_power - 1.0) * omori_offset ** (omori_power - 1.0) / (2.0 * math.pi)
    area = spread_ref[...] * spread_ref[...]
    l_ref[...] = jnp.log(prod_ref[...] * norm / area) * LOG2E
    v_ref[...] = (0.5 * cell_km * cell_km * LOG2E) / area
    events = t_ref.shape[1]
    shape = (out_ref.shape[0], 1, events)
    for k, ref in enumerate([t_ref, r_ref, c_ref, m_ref, b_ref]):
        row = ref[...].astype(jnp.float32)
        out_ref[:, :, k * events : (k + 1) * events] = jnp.broadcast_to(row[None], shape)


def kernel(g_ref, lof_ref, vof_ref, logint_ref, dens_ref,
           all_s, own_s, blk_v, fst_v, blk_s, fst_s, sel_s, dep_s, a_buf, b_buf, x_s, sems):
    f32 = jnp.float32
    bf16 = jnp.bfloat16
    i32 = jnp.int32
    blocks = g_ref.shape[0]
    events = g_ref.shape[2] // 5
    halves = events // LANES
    nbin = lof_ref.shape[1]
    listed = blk_v.shape[1]
    tall = 8
    own = lax.axis_index("tm") * lax.axis_size("grid") + lax.axis_index("grid")
    first_row = (own * LATITUDE_SPAN).astype(f32)

    l_of = lof_ref[...]
    v_of = vof_ref[...]

    def fields(k, carry):
        at = pl.ds(pl.multiple_of(k * tall, tall), tall)
        times = g_ref[at, 0, 0:events]
        rows = g_ref[at, 0, events : 2 * events]
        cols = g_ref[at, 0, 2 * events : 3 * events]
        base = g_ref[at, 0, 4 * events : 5 * events]
        mag = g_ref[at, 0, 3 * events : 4 * events]
        need = (rows >= first_row - rim_width) & (
            rows <= first_row + (LATITUDE_SPAN - 1 + rim_width)
        )
        l_j = jnp.broadcast_to(l_of[:, 0:1], mag.shape)
        v_j = jnp.broadcast_to(v_of[:, 0:1], mag.shape)
        for n in range(1, nbin):
            hit = mag == float(n)
            l_j = jnp.where(hit, l_of[:, n : n + 1], l_j)
            v_j = jnp.where(hit, v_of[:, n : n + 1], v_j)
        need_f = jnp.where(need, 1.0, 0.0)
        for f, value in ((T, times), (R, rows), (C, cols), (L, l_j), (V, v_j), (B, base), (PICK, need_f)):
            all_s[f, at] = value
        return carry

    lax.fori_loop(0, blocks // tall, fields, 0)
    pad = (tall, events)
    start = jnp.broadcast_to(g_ref[0:1, 0, 0:1], pad)
    zeros = jnp.zeros(pad, f32)
    for f, value in ((T, start), (R, zeros), (C, zeros), (L, jnp.full(pad, -1e30, f32)), (V, zeros)):
        all_s[f, blocks : blocks + tall] = value

    need_f = all_s[PICK, 0:blocks]
    upper = lax.broadcasted_iota(i32, (events, events), 0) <= lax.broadcasted_iota(
        i32, (events, events), 1
    )
    upper = jnp.where(upper, 1.0, 0.0).astype(bf16)
    pos = jnp.dot(need_f.astype(bf16), upper, preferred_element_type=f32)
    all_s[RANK, 0:blocks] = pos
    all_s[PICK, 0:blocks] = need_f * pos

    count = jnp.sum(need_f, axis=1, keepdims=True)
    units = jnp.floor((count + (UNIT - 1)) * (1.0 / UNIT))
    lower = lax.broadcasted_iota(i32, (blocks, blocks), 0) >= lax.broadcasted_iota(
        i32, (blocks, blocks), 1
    )
    ends = jnp.dot(
        jnp.where(lower, 1.0, 0.0).astype(bf16),
        jnp.broadcast_to(units, (blocks, LANES)).astype(bf16),
        preferred_element_type=f32,
    )
    lane = lax.broadcasted_iota(i32, (1, LANES), 1)
    beyond = 1e6

    def list_part(k, carry):
        at = k * LANES
        if not isinstance(k, int):
            at = pl.multiple_of(at, LANES)
        u = (lane + at).astype(f32)
        done = ends <= u
        blk = jnp.sum(jnp.where(done, 1.0, 0.0), axis=0, keepdims=True)
        start = jnp.max(jnp.where(done, ends, 0.0), axis=0, keepdims=True)
        last = float(blocks - 1)
        blk_v[:, pl.ds(at, LANES)] = jnp.minimum(blk, last).astype(i32)
        fst_v[:, pl.ds(at, LANES)] = (u - start) * float(UNIT) + jnp.where(blk > last, beyond, 0.0)
        return carry

    if listed <= 16 * LANES:
        for k in range(listed // LANES):
            list_part(k, 0)
    else:
        lax.fori_loop(0, listed // LANES, list_part, 0)
    copies = [
        pltpu.make_async_copy(blk_v, blk_s, sems.at[0]),
        pltpu.make_async_copy(fst_v, fst_s, sems.at[1]),
    ]
    for copy in copies:
        copy.start()

    def row_of(b):
        def part(field, h):
            return all_s[field, pl.ds(b, 1), :][:, h * LANES : (h + 1) * LANES]

        return part

    def lane_sums(t_i, r_i, c_i, b, before):
        total = None
        for back in range(NB + 1):
            part = row_of(b if back == 0 else jnp.where(b >= back, b - back, blocks))
            for h in range(halves):
                gap = (t_i - part(T, h)) + omori_offset
                dr = r_i - part(R, h)
                dc = c_i - part(C, h)
                expo = (part(L, h) - (omori_power * LOG2E) * jnp.log(gap)) - (
                    dr * dr + dc * dc
                ) * part(V, h)
                term = jnp.exp2(expo)
                if back == 0:
                    term = jnp.where(before(part, h), term, 0.0)
                total = term if total is None else total + term
        return jnp.sum(total, axis=1, keepdims=True)

    sub_f = lax.broadcasted_iota(i32, (UNIT, LANES), 0).astype(f32)
    lane_f = lax.broadcasted_iota(i32, (UNIT, LANES), 1).astype(f32)
    own_rows = jnp.concatenate(
        [g_ref[own, 0:1, k * events : (k + 1) * events] for k in range(3)]
        + [jnp.zeros((5, events), f32)]
    )
    own_cols = jnp.transpose(own_rows)
    for k in range(3):
        own_s[k] = jnp.broadcast_to(own_cols[:, k : k + 1], (events, LANES))

    own_steps = events // (OWN_STEP * UNIT)
    dep_s[...] = jnp.zeros_like(dep_s)

    def own_step(k, found):
        for ref, first, size in ((x_s, 8, M_ROWS), (a_buf, 0, a_buf.shape[0]), (b_buf, 0, b_buf.shape[0])):
            size = size // own_steps
            at = pl.ds(pl.multiple_of(first + k * size, 8), size)
            ref[at] = jnp.zeros((size, ref.shape[1]), ref.dtype)
        for j in range(OWN_STEP):
            at = k * (OWN_STEP * UNIT) + j * UNIT
            target = sub_f + at.astype(f32)
            t_i, r_i, c_i = (own_s[n, pl.ds(pl.multiple_of(at, UNIT), UNIT)] for n in range(3))
            trig = lane_sums(t_i, r_i, c_i, own, lambda part, h: lane_f + h * LANES < target)
            found = tuple(
                found[h] + jnp.where(lane_f + h * LANES == target, trig, 0.0) for h in range(halves)
            )
        return found

    found = lax.fori_loop(
        0, own_steps, own_step, tuple(jnp.zeros((UNIT, LANES), f32) for _ in range(halves))
    )
    for h in range(halves):
        trig = jnp.sum(found[h], axis=0, keepdims=True)
        logint_ref[:, h * LANES : (h + 1) * LANES] = jnp.log(row_of(own)(B, h) + trig)

    for copy in copies:
        copy.wait()
    total_units = (listed - 1) - ((fst_s[0, listed - 1] - beyond) * (1.0 / UNIT)).astype(i32)

    rank = sub_f + 1.0
    slots = STEP * UNIT
    steps = BATCH // slots
    lane_s = lax.broadcasted_iota(i32, (slots, LANES), 1)
    m_row = (lane_s % LATITUDE_SPAN).astype(f32)
    col_blocks = M_ROWS // LATITUDE_SPAN
    m_hi = []
    for h in range(M_ROWS // LANES):
        m = lane_s + h * LANES
        m_hi.append((m // LATITUDE_SPAN % 2 * (col_blocks // 2) + m // (2 * LATITUDE_SPAN)).astype(FT))
    l_lo = [(lane_s + h * LANES).astype(FT) for h in range(LO_COLS // LANES)]
    zero, one = jnp.zeros((), FT), jnp.ones((), FT)

    def flush(size):
        x_s[8 : 8 + M_ROWS] += lax.dot_general(
            a_buf[0:size], b_buf[0:size], (((0,), (0,)), ((), ())), preferred_element_type=f32
        )

    def factors(slot):
        r_i, c_i, b_i, trig = dep_s[0], dep_s[1], dep_s[2], dep_s[3]
        share = jnp.where(b_i > 0.0, b_i / (b_i + trig), 0.0)
        share = share.astype(bf16).astype(f32)
        hi = jnp.floor(c_i * (1.0 / LO_COLS))
        lo = (c_i - hi * LO_COLS).astype(FT)
        hi = hi.astype(FT)
        d = m_row - (r_i - first_row)
        d2 = d * d
        w = jnp.exp2(d2 * (-LOG2E / (2.0 * smooth_sigma**2))) * share
        w = jnp.where(d2 < (rim_width + 0.5) ** 2, w, 0.0).astype(FT)
        at = pl.ds(pl.multiple_of(slot * slots, slots), slots)
        for h in range(M_ROWS // LANES):
            a_buf[at, h * LANES : (h + 1) * LANES] = jnp.where(m_hi[h] == hi, w, zero).astype(bf16)
        for h in range(LO_COLS // LANES):
            b_buf[at, h * LANES : (h + 1) * LANES] = jnp.where(l_lo[h] == lo, one, zero).astype(bf16)

    def unit_triggers(i):
        for j in range(STEP):
            u = i * STEP + j
            b = blk_s[0, u]
            order = rank + fst_s[0, u]
            at = slice(j * UNIT, (j + 1) * UNIT)
            t_i, r_i, c_i = sel_s[0, at], sel_s[1, at], sel_s[2, at]
            trig = lane_sums(t_i, r_i, c_i, b, lambda part, h: part(RANK, h) < order)
            dep_s[0, at] = r_i
            dep_s[1, at] = c_i
            dep_s[2, at] = sel_s[3, at]
            dep_s[3, at] = jnp.broadcast_to(trig, (UNIT, LANES))

    def pick_events(i):
        for j in range(STEP):
            u = i * STEP + j
            b = blk_s[0, u]
            order = rank + fst_s[0, u]
            part = row_of(b)
            picks = [part(PICK, h) == order for h in range(halves)]
            for k, field in enumerate((T, R, C, B)):
                value = None
                for h in range(halves):
                    piece = jnp.where(picks[h], part(field, h), 0.0)
                    value = piece if value is None else value + piece
                value = jnp.sum(value, axis=1, keepdims=True)
                sel_s[k, j * UNIT : (j + 1) * UNIT] = jnp.broadcast_to(value, (UNIT, LANES))

    total_steps = (total_units + (STEP - 1)) // STEP
    pick_events(0)

    def batch(q, carry):
        @pl.when(q > 0)
        def _():
            flush(BATCH)
            a_buf[...] = jnp.zeros_like(a_buf)

        def step(k, carry):
            i = q * steps + k
            factors(k)
            unit_triggers(i)
            pick_events(i + 1)
            return carry

        return lax.fori_loop(0, jnp.minimum(total_steps - q * steps, steps), step, 0)

    batches = (total_steps + (steps - 1)) // steps
    lax.fori_loop(0, batches, batch, 0)
    factors(total_steps - jnp.maximum(batches - 1, 0) * steps)
    flush(BATCH + slots)

    span = LATITUDE_SPAN
    wide = LO_COLS // LANES
    middle = (col_blocks // 2) * LO_COLS
    edge = jnp.zeros((span, LO_COLS), f32)
    x_s[0:8] = jnp.concatenate([edge, x_s[M_ROWS : M_ROWS + span]])
    x_s[8 + M_ROWS : 16 + M_ROWS] = jnp.concatenate([x_s[8 + span : 16], edge])
    lane_t = lax.broadcasted_iota(i32, (8, LANES), 1)
    per = PER

    def columns(g, carry):
        for p in range(per):
            m = g * (8 * per) + 8 * p

            def tile(shift, h):
                return x_s[pl.ds(pl.multiple_of(m + 8 + shift, 8), 8), h * LANES : (h + 1) * LANES]

            mids = [tile(0, h) for h in range(wide)]
            lefts = [tile(-8, wide - 1)] + mids[:-1]
            rights = mids[1:] + [tile(8, 0)]
            for h in range(wide):
                acc = mids[h] * (WEIGHTS[rim_width] / WEIGHT_SUM**2)
                for b in range(1, rim_width + 1):
                    from_left = pltpu.roll(jnp.where(lane_t >= LANES - b, lefts[h], mids[h]), b, 1)
                    from_right = pltpu.roll(jnp.where(lane_t < b, rights[h], mids[h]), LANES - b, 1)
                    acc = acc + (from_left + from_right) * (WEIGHTS[rim_width + b] / WEIGHT_SUM**2)
                at = (g * per + p) * LO_COLS + h * LANES
                for half in range(2):
                    place = pl.ds(pl.multiple_of(at + half * middle, LANES), LANES)
                    dens_ref[:, place] = acc[half * span : (half + 1) * span]
        return carry

    lax.fori_loop(0, M_ROWS // (8 * per), columns, 0)


def body(times, cell_row, cell_col, magnitude, base_rate, productivity, spread):
    events = times.shape[0]
    blocks = lax.axis_size(AXES)
    f32 = jnp.float32
    rows = [x.reshape(1, events) for x in (times, cell_row, cell_col, magnitude, base_rate)]
    vmem = pl.BlockSpec(memory_space=pltpu.VMEM)
    rows += [x.reshape(1, -1) for x in (productivity, spread)]
    table = jax.ShapeDtypeStruct((1, productivity.shape[0]), f32)
    spread_out, l_table, v_table = pl.pallas_call(
        spread_kernel,
        out_shape=(jax.ShapeDtypeStruct((blocks, 1, 5 * events), f32), table, table),
        in_specs=[vmem] * 7,
        out_specs=(vmem, vmem, vmem),
        compiler_params=pltpu.CompilerParams(vmem_limit_bytes=16 * MIB),
    )(*rows)
    gathered = lax.all_to_all(spread_out, AXES, 0, 0, tiled=True)
    listed = blocks * events // UNIT + LANES
    log_intensity, density = pl.pallas_call(
        kernel,
        out_shape=(
            jax.ShapeDtypeStruct((1, events), f32),
            jax.ShapeDtypeStruct((LATITUDE_SPAN, COLS), f32),
        ),
        in_specs=[vmem, vmem, vmem],
        out_specs=(vmem, vmem),
        scratch_shapes=[
            pltpu.VMEM((FIELDS, blocks + 8, events), f32),
            pltpu.VMEM((3, events, LANES), f32),
            pltpu.VMEM((1, listed), jnp.int32),
            pltpu.VMEM((1, listed), f32),
            pltpu.SMEM((1, listed), jnp.int32),
            pltpu.SMEM((1, listed), f32),
            pltpu.VMEM((4, STEP * UNIT, LANES), f32),
            pltpu.VMEM((4, STEP * UNIT, LANES), f32),
            pltpu.VMEM((BATCH + STEP * UNIT, M_ROWS), jnp.bfloat16),
            pltpu.VMEM((BATCH + STEP * UNIT, LO_COLS), jnp.bfloat16),
            pltpu.VMEM((M_ROWS + 16, LO_COLS), f32),
            pltpu.SemaphoreType.DMA((2,)),
        ],
        compiler_params=pltpu.CompilerParams(vmem_limit_bytes=32 * MIB),
    )(gathered, l_table, v_table)
    return (log_intensity.reshape(events), density)


def solution(mesh):
    in_specs = (P(AXES), P(AXES), P(AXES), P(AXES), P(AXES), P(), P())
    out_specs = (P(AXES), P(AXES, None))
    return jax.shard_map(body, mesh=mesh, in_specs=in_specs, out_specs=out_specs, check_vma=False)
```

```python
import math

import jax
import jax.numpy as jnp
from jax import lax
from jax.experimental import pallas as pl
from jax.experimental.pallas import tpu as pltpu
from jax.sharding import PartitionSpec as P

NB = 2
LATITUDE_SPAN = 4
COLS = 16384

omori_power = 1.2
omori_offset = 0.5
cell_km = 0.1
smooth_sigma = 1.5
rim_width = 3

AXES = ("tm", "grid")
LANES = 128
UNIT = 8
STEP = 16
FINAL = 1
LO_COLS = 256
M_ROWS = LATITUDE_SPAN * (COLS // LO_COLS)
LOG2E = math.log2(math.e)
WEIGHTS = [math.exp(-(b * b) / (2.0 * smooth_sigma**2)) for b in range(-rim_width, rim_width + 1)]
WEIGHT_SUM = sum(WEIGHTS)
MIB = 1 << 20
FIELDS = 8
T, R, C, L, V, B, RANK, PICK = range(FIELDS)
FT = jnp.bfloat16


def spread_kernel(t_ref, r_ref, c_ref, m_ref, b_ref, prod_ref, spread_ref, out_ref, l_ref, v_ref):
    norm = (omori_power - 1.0) * omori_offset ** (omori_power - 1.0) / (2.0 * math.pi)
    area = spread_ref[...] * spread_ref[...]
    l_ref[...] = jnp.log(prod_ref[...] * norm / area) * LOG2E
    v_ref[...] = (0.5 * cell_km * cell_km * LOG2E) / area
    events = t_ref.shape[1]
    shape = (out_ref.shape[0], 1, events)
    for k, ref in enumerate([t_ref, r_ref, c_ref, m_ref, b_ref]):
        row = ref[...].astype(jnp.float32)
        out_ref[:, :, k * events : (k + 1) * events] = jnp.broadcast_to(row[None], shape)


def kernel(g_ref, lof_ref, vof_ref, logint_ref, dens_ref,
           all_s, own_s, blk_v, fst_v, blk_s, fst_s, sel_s, dep_s, a_buf, b_buf, x_s, sems):
    f32 = jnp.float32
    bf16 = jnp.bfloat16
    i32 = jnp.int32
    blocks = g_ref.shape[0]
    events = g_ref.shape[2] // 5
    halves = events // LANES
    nbin = lof_ref.shape[1]
    listed = blk_v.shape[1]
    tall = 8
    own = lax.axis_index("tm") * lax.axis_size("grid") + lax.axis_index("grid")
    first_row = (own * LATITUDE_SPAN).astype(f32)

    all_rows = g_ref[:, 0, events : 2 * events]
    need = (all_rows >= first_row - rim_width) & (
        all_rows <= first_row + (LATITUDE_SPAN - 1 + rim_width)
    )
    need_f = jnp.where(need, 1.0, 0.0)
    all_s[PICK, 0:blocks] = need_f

    count = jnp.sum(need_f, axis=1, keepdims=True)
    units = jnp.floor((count + (UNIT - 1)) * (1.0 / UNIT))
    lower = lax.broadcasted_iota(i32, (blocks, blocks), 0) >= lax.broadcasted_iota(
        i32, (blocks, blocks), 1
    )
    ends = jnp.dot(
        jnp.where(lower, 1.0, 0.0).astype(bf16),
        jnp.broadcast_to(units, (blocks, LANES)).astype(bf16),
        preferred_element_type=f32,
    )
    lane = lax.broadcasted_iota(i32, (1, LANES), 1)
    beyond = 1e6

    def list_part(k, carry):
        at = k * LANES
        if not isinstance(k, int):
            at = pl.multiple_of(at, LANES)
        u = (lane + at).astype(f32)
        done = ends <= u
        blk = jnp.sum(jnp.where(done, 1.0, 0.0), axis=0, keepdims=True)
        start = jnp.max(jnp.where(done, ends, 0.0), axis=0, keepdims=True)
        last = float(blocks - 1)
        blk_v[:, pl.ds(at, LANES)] = jnp.minimum(blk, last).astype(i32)
        fst_v[:, pl.ds(at, LANES)] = (u - start) * float(UNIT) + jnp.where(blk > last, beyond, 0.0)
        return carry

    if listed <= 16 * LANES:
        for k in range(listed // LANES):
            list_part(k, 0)
    else:
        lax.fori_loop(0, listed // LANES, list_part, 0)
    copies = [
        pltpu.make_async_copy(blk_v, blk_s, sems.at[0]),
        pltpu.make_async_copy(fst_v, fst_s, sems.at[1]),
    ]
    for copy in copies:
        copy.start()

    l_of = lof_ref[...]
    v_of = vof_ref[...]

    def fields(k, carry):
        at = pl.ds(pl.multiple_of(k * tall, tall), tall)
        times = g_ref[at, 0, 0:events]
        rows = g_ref[at, 0, events : 2 * events]
        cols = g_ref[at, 0, 2 * events : 3 * events]
        base = g_ref[at, 0, 4 * events : 5 * events]
        mag = g_ref[at, 0, 3 * events : 4 * events]
        l_j = jnp.broadcast_to(l_of[:, 0:1], mag.shape)
        v_j = jnp.broadcast_to(v_of[:, 0:1], mag.shape)
        for n in range(1, nbin):
            hit = mag == float(n)
            l_j = jnp.where(hit, l_of[:, n : n + 1], l_j)
            v_j = jnp.where(hit, v_of[:, n : n + 1], v_j)
        for f, value in ((T, times), (R, rows), (C, cols), (L, l_j), (V, v_j), (B, base)):
            all_s[f, at] = value
        return carry

    lax.fori_loop(0, blocks // tall, fields, 0)

    def clear(k, carry):
        for ref, first, size in ((x_s, 8, M_ROWS), (a_buf, 0, a_buf.shape[0]), (b_buf, 0, b_buf.shape[0])):
            at = pl.ds(pl.multiple_of(first + k * (size // 4), 8), size // 4)
            ref[at] = jnp.zeros((size // 4, ref.shape[1]), ref.dtype)
        return carry

    lax.fori_loop(0, 4, clear, 0)
    pad = (tall, events)
    start = jnp.broadcast_to(g_ref[0:1, 0, 0:1], pad)
    zeros = jnp.zeros(pad, f32)
    for f, value in ((T, start), (R, zeros), (C, zeros), (L, jnp.full(pad, -1e30, f32)), (V, zeros)):
        all_s[f, blocks : blocks + tall] = value

    need_f = all_s[PICK, 0:blocks]
    upper = lax.broadcasted_iota(i32, (events, events), 0) <= lax.broadcasted_iota(
        i32, (events, events), 1
    )
    upper = jnp.where(upper, 1.0, 0.0).astype(bf16)
    pos = jnp.dot(need_f.astype(bf16), upper, preferred_element_type=f32)
    all_s[RANK, 0:blocks] = pos
    all_s[PICK, 0:blocks] = need_f * pos

    def row_of(b):
        def part(field, h):
            return all_s[field, pl.ds(b, 1), :][:, h * LANES : (h + 1) * LANES]

        return part

    def lane_sums(t_i, r_i, c_i, b, before):
        total = None
        for back in range(NB + 1):
            part = row_of(b if back == 0 else jnp.where(b >= back, b - back, blocks))
            for h in range(halves):
                gap = (t_i - part(T, h)) + omori_offset
                dr = r_i - part(R, h)
                dc = c_i - part(C, h)
                expo = (part(L, h) - (omori_power * LOG2E) * jnp.log(gap)) - (
                    dr * dr + dc * dc
                ) * part(V, h)
                term = jnp.exp2(expo)
                if back == 0:
                    term = jnp.where(before(part, h), term, 0.0)
                total = term if total is None else total + term
        return jnp.sum(total, axis=1, keepdims=True)

    sub_f = lax.broadcasted_iota(i32, (UNIT, LANES), 0).astype(f32)
    lane_f = lax.broadcasted_iota(i32, (UNIT, LANES), 1).astype(f32)
    own_rows = jnp.concatenate(
        [g_ref[own, 0:1, k * events : (k + 1) * events] for k in range(3)]
        + [jnp.zeros((5, events), f32)]
    )
    own_cols = jnp.transpose(own_rows)
    for k in range(3):
        own_s[k] = jnp.broadcast_to(own_cols[:, k : k + 1], (events, LANES))

    dep_s[2] = jnp.zeros_like(dep_s[2])

    for copy in copies:
        copy.wait()
    total_units = (listed - 1) - ((fst_s[0, listed - 1] - beyond) * (1.0 / UNIT)).astype(i32)

    rank = sub_f + 1.0
    slots = STEP * UNIT
    lane_s = lax.broadcasted_iota(i32, (slots, LANES), 1)
    m_row = (lane_s % LATITUDE_SPAN).astype(f32)
    col_blocks = M_ROWS // LATITUDE_SPAN
    m_hi = []
    for h in range(M_ROWS // LANES):
        m = lane_s + h * LANES
        m_hi.append((m // LATITUDE_SPAN % 2 * (col_blocks // 2) + m // (2 * LATITUDE_SPAN)).astype(FT))
    l_lo = [(lane_s + h * LANES).astype(FT) for h in range(LO_COLS // LANES)]
    zero, one = jnp.zeros((), FT), jnp.ones((), FT)

    def flush(size):
        x_s[8 : 8 + M_ROWS] += lax.dot_general(
            a_buf[0:size], b_buf[0:size], (((0,), (0,)), ((), ())), preferred_element_type=f32
        )

    def factors(slot):
        r_i, c_i, b_i, trig = dep_s[0], dep_s[1], dep_s[2], dep_s[3]
        share = jnp.where(b_i > 0.0, b_i / (b_i + trig), 0.0)
        share = share.astype(bf16).astype(f32)
        hi = jnp.floor(c_i * (1.0 / LO_COLS))
        lo = (c_i - hi * LO_COLS).astype(FT)
        hi = hi.astype(FT)
        d = m_row - (r_i - first_row)
        d2 = d * d
        w = jnp.exp2(d2 * (-LOG2E / (2.0 * smooth_sigma**2))) * share
        w = jnp.where(d2 < (rim_width + 0.5) ** 2, w, 0.0).astype(FT)
        at = slice(slot * slots, (slot + 1) * slots)
        for h in range(M_ROWS // LANES):
            a_buf[at, h * LANES : (h + 1) * LANES] = jnp.where(m_hi[h] == hi, w, zero).astype(bf16)
        for h in range(LO_COLS // LANES):
            b_buf[at, h * LANES : (h + 1) * LANES] = jnp.where(l_lo[h] == lo, one, zero).astype(bf16)

    def unit_triggers(i):
        for j in range(STEP):
            u = i * STEP + j
            b = blk_s[0, u]
            order = rank + fst_s[0, u]
            at = slice(j * UNIT, (j + 1) * UNIT)
            t_i, r_i, c_i = sel_s[0, at], sel_s[1, at], sel_s[2, at]
            trig = lane_sums(t_i, r_i, c_i, b, lambda part, h: part(RANK, h) < order)
            dep_s[0, at] = r_i
            dep_s[1, at] = c_i
            dep_s[2, at] = sel_s[3, at]
            dep_s[3, at] = jnp.broadcast_to(trig, (UNIT, LANES))

    def pick_events(i):
        for j in range(STEP):
            u = i * STEP + j
            b = blk_s[0, u]
            order = rank + fst_s[0, u]
            part = row_of(b)
            picks = [part(PICK, h) == order for h in range(halves)]
            for k, field in enumerate((T, R, C, B)):
                value = None
                for h in range(halves):
                    piece = jnp.where(picks[h], part(field, h), 0.0)
                    value = piece if value is None else value + piece
                value = jnp.sum(value, axis=1, keepdims=True)
                sel_s[k, j * UNIT : (j + 1) * UNIT] = jnp.broadcast_to(value, (UNIT, LANES))

    total_steps = (total_units + (STEP - 1)) // STEP
    pick_events(0)

    def step(i, carry):
        flush(slots)
        factors(0)
        unit_triggers(i)
        pick_events(i + 1)
        return carry

    lax.fori_loop(0, total_steps, step, 0)
    factors(1)
    flush(2 * slots)

    span = LATITUDE_SPAN
    wide = LO_COLS // LANES
    middle = (col_blocks // 2) * LO_COLS
    edge = jnp.zeros((span, LO_COLS), f32)
    x_s[0:8] = jnp.concatenate([edge, x_s[M_ROWS : M_ROWS + span]])
    x_s[8 + M_ROWS : 16 + M_ROWS] = jnp.concatenate([x_s[8 + span : 16], edge])
    lane_t = lax.broadcasted_iota(i32, (8, LANES), 1)
    per = M_ROWS // (8 * FINAL)
    own_per = events // (UNIT * FINAL)

    def rows_at(at):
        return slice(at, at + UNIT) if isinstance(at, int) else pl.ds(pl.multiple_of(at, UNIT), UNIT)

    def columns(g, carry):
        for p in range(per):
            for j in range(p * own_per // per, (p + 1) * own_per // per):
                at = g * (own_per * UNIT) + j * UNIT
                target = sub_f + float(at) if isinstance(at, int) else sub_f + at.astype(f32)
                t_i, r_i, c_i = (own_s[n, rows_at(at)] for n in range(3))
                trig = lane_sums(t_i, r_i, c_i, own, lambda part, h: lane_f + h * LANES < target)
                own_s[3, rows_at(at)] = jnp.broadcast_to(trig, (UNIT, LANES))
            m = g * (8 * per) + 8 * p

            def tile(shift, h):
                return x_s[rows_at(m + 8 + shift), h * LANES : (h + 1) * LANES]

            mids = [tile(0, h) for h in range(wide)]
            lefts = [tile(-8, wide - 1)] + mids[:-1]
            rights = mids[1:] + [tile(8, 0)]
            for h in range(wide):
                acc = mids[h] * (WEIGHTS[rim_width] / WEIGHT_SUM**2)
                for b in range(1, rim_width + 1):
                    from_left = pltpu.roll(jnp.where(lane_t >= LANES - b, lefts[h], mids[h]), b, 1)
                    from_right = pltpu.roll(jnp.where(lane_t < b, rights[h], mids[h]), LANES - b, 1)
                    acc = acc + (from_left + from_right) * (WEIGHTS[rim_width + b] / WEIGHT_SUM**2)
                at = (g * per + p) * LO_COLS + h * LANES
                for half in range(2):
                    place = at + half * middle
                    place = slice(place, place + LANES) if isinstance(place, int) else pl.ds(pl.multiple_of(place, LANES), LANES)
                    dens_ref[:, place] = acc[half * span : (half + 1) * span]
        return carry

    if FINAL == 1:
        columns(0, 0)
    else:
        lax.fori_loop(0, FINAL, columns, 0)
    for h in range(halves):
        found = own_s[3, h * LANES : (h + 1) * LANES]
        diagonal = lax.broadcasted_iota(i32, (LANES, LANES), 0) == lax.broadcasted_iota(
            i32, (LANES, LANES), 1
        )
        trig = jnp.sum(jnp.where(diagonal, found, 0.0), axis=0, keepdims=True)
        logint_ref[:, h * LANES : (h + 1) * LANES] = jnp.log(row_of(own)(B, h) + trig)


def body(times, cell_row, cell_col, magnitude, base_rate, productivity, spread):
    events = times.shape[0]
    blocks = lax.axis_size(AXES)
    f32 = jnp.float32
    rows = [x.reshape(1, events) for x in (times, cell_row, cell_col, magnitude, base_rate)]
    vmem = pl.BlockSpec(memory_space=pltpu.VMEM)
    rows += [x.reshape(1, -1) for x in (productivity, spread)]
    table = jax.ShapeDtypeStruct((1, productivity.shape[0]), f32)
    spread_out, l_table, v_table = pl.pallas_call(
        spread_kernel,
        out_shape=(jax.ShapeDtypeStruct((blocks, 1, 5 * events), f32), table, table),
        in_specs=[vmem] * 7,
        out_specs=(vmem, vmem, vmem),
        compiler_params=pltpu.CompilerParams(vmem_limit_bytes=16 * MIB),
    )(*rows)
    gathered = lax.all_to_all(spread_out, AXES, 0, 0, tiled=True)
    listed = blocks * events // UNIT + LANES
    log_intensity, density = pl.pallas_call(
        kernel,
        out_shape=(
            jax.ShapeDtypeStruct((1, events), f32),
            jax.ShapeDtypeStruct((LATITUDE_SPAN, COLS), f32),
        ),
        in_specs=[vmem, vmem, vmem],
        out_specs=(vmem, vmem),
        scratch_shapes=[
            pltpu.VMEM((FIELDS, blocks + 8, events), f32),
            pltpu.VMEM((4, events, LANES), f32),
            pltpu.VMEM((1, listed), jnp.int32),
            pltpu.VMEM((1, listed), f32),
            pltpu.SMEM((1, listed), jnp.int32),
            pltpu.SMEM((1, listed), f32),
            pltpu.VMEM((4, STEP * UNIT, LANES), f32),
            pltpu.VMEM((4, STEP * UNIT, LANES), f32),
            pltpu.VMEM((2 * STEP * UNIT, M_ROWS), jnp.bfloat16),
            pltpu.VMEM((2 * STEP * UNIT, LO_COLS), jnp.bfloat16),
            pltpu.VMEM((M_ROWS + 16, LO_COLS), f32),
            pltpu.SemaphoreType.DMA((2,)),
        ],
        compiler_params=pltpu.CompilerParams(vmem_limit_bytes=32 * MIB),
    )(gathered, l_table, v_table)
    return (log_intensity.reshape(events), density)


def solution(mesh):
    in_specs = (P(AXES), P(AXES), P(AXES), P(AXES), P(AXES), P(), P())
    out_specs = (P(AXES), P(AXES, None))
    return jax.shard_map(body, mesh=mesh, in_specs=in_specs, out_specs=out_specs, check_vma=False)
```

```python
import math

import jax
import jax.numpy as jnp
from jax import lax
from jax.experimental import pallas as pl
from jax.experimental.pallas import tpu as pltpu
from jax.sharding import PartitionSpec as P

NB = 2
LATITUDE_SPAN = 4
COLS = 16384

omori_power = 1.2
omori_offset = 0.5
cell_km = 0.1
smooth_sigma = 1.5
rim_width = 3

AXES = ("tm", "grid")
LANES = 128
SPLIT = 8
UNIT = 8
STEP = 16
FINAL = 1
LO_COLS = 256
M_ROWS = LATITUDE_SPAN * (COLS // LO_COLS)
LOG2E = math.log2(math.e)
WEIGHTS = [math.exp(-(b * b) / (2.0 * smooth_sigma**2)) for b in range(-rim_width, rim_width + 1)]
WEIGHT_SUM = sum(WEIGHTS)
MIB = 1 << 20
FIELDS = 8
T, R, C, L, V, B, RANK, PICK = range(FIELDS)
FT = jnp.bfloat16


def spread_kernel(t_ref, r_ref, c_ref, m_ref, b_ref, prod_ref, spread_ref, out_ref, l_ref, v_ref):
    norm = (omori_power - 1.0) * omori_offset ** (omori_power - 1.0) / (2.0 * math.pi)
    area = spread_ref[...] * spread_ref[...]
    l_ref[...] = jnp.log(prod_ref[...] * norm / area) * LOG2E
    v_ref[...] = (0.5 * cell_km * cell_km * LOG2E) / area
    events = t_ref.shape[1]
    shape = (out_ref.shape[0], 1, events)
    for k, ref in enumerate([t_ref, r_ref, c_ref, m_ref, b_ref]):
        row = ref[...].astype(jnp.float32)
        out_ref[:, :, k * events : (k + 1) * events] = jnp.broadcast_to(row[None], shape)


def kernel(g_ref, lof_ref, vof_ref, logint_ref, dens_ref,
           all_s, own_s, blk_v, fst_v, blk_s, fst_s, sel_s, dep_s, a_buf, b_buf, x_s, sems):
    f32 = jnp.float32
    bf16 = jnp.bfloat16
    i32 = jnp.int32
    runs = g_ref.shape[1]
    blocks = SPLIT * runs
    events = g_ref.shape[3] // 5
    halves = events // LANES
    nbin = lof_ref.shape[1]
    listed = blk_v.shape[1]
    tall = SPLIT
    own = lax.axis_index("tm") * lax.axis_size("grid") + lax.axis_index("grid")
    first_row = (own * LATITUDE_SPAN).astype(f32)

    all_rows = jnp.concatenate(
        [g_ref[:, k, 0, events : 2 * events] for k in range(runs)]
    )
    need = (all_rows >= first_row - rim_width) & (
        all_rows <= first_row + (LATITUDE_SPAN - 1 + rim_width)
    )
    need_f = jnp.where(need, 1.0, 0.0)
    all_s[PICK, 0:blocks] = need_f

    count = jnp.sum(need_f, axis=1, keepdims=True)
    units = jnp.floor((count + (UNIT - 1)) * (1.0 / UNIT))
    lower = lax.broadcasted_iota(i32, (blocks, blocks), 0) >= lax.broadcasted_iota(
        i32, (blocks, blocks), 1
    )
    ends = jnp.dot(
        jnp.where(lower, 1.0, 0.0).astype(bf16),
        jnp.broadcast_to(units, (blocks, LANES)).astype(bf16),
        preferred_element_type=f32,
    )
    lane = lax.broadcasted_iota(i32, (1, LANES), 1)
    beyond = 1e6

    def list_part(k, carry):
        at = k * LANES
        if not isinstance(k, int):
            at = pl.multiple_of(at, LANES)
        u = (lane + at).astype(f32)
        done = ends <= u
        blk = jnp.sum(jnp.where(done, 1.0, 0.0), axis=0, keepdims=True)
        start = jnp.max(jnp.where(done, ends, 0.0), axis=0, keepdims=True)
        last = float(blocks - 1)
        blk_v[:, pl.ds(at, LANES)] = jnp.minimum(blk, last).astype(i32)
        fst_v[:, pl.ds(at, LANES)] = (u - start) * float(UNIT) + jnp.where(blk > last, beyond, 0.0)
        return carry

    if listed <= 16 * LANES:
        for k in range(listed // LANES):
            list_part(k, 0)
    else:
        lax.fori_loop(0, listed // LANES, list_part, 0)
    copies = [
        pltpu.make_async_copy(blk_v, blk_s, sems.at[0]),
        pltpu.make_async_copy(fst_v, fst_s, sems.at[1]),
    ]
    for copy in copies:
        copy.start()

    l_of = lof_ref[...]
    v_of = vof_ref[...]

    def fields(k, carry):
        at = pl.ds(pl.multiple_of(k * tall, tall), tall)
        times = g_ref[:, k, 0, 0:events]
        rows = g_ref[:, k, 0, events : 2 * events]
        cols = g_ref[:, k, 0, 2 * events : 3 * events]
        base = g_ref[:, k, 0, 4 * events : 5 * events]
        mag = g_ref[:, k, 0, 3 * events : 4 * events]
        l_j = jnp.broadcast_to(l_of[:, 0:1], mag.shape)
        v_j = jnp.broadcast_to(v_of[:, 0:1], mag.shape)
        for n in range(1, nbin):
            hit = mag == float(n)
            l_j = jnp.where(hit, l_of[:, n : n + 1], l_j)
            v_j = jnp.where(hit, v_of[:, n : n + 1], v_j)
        for f, value in ((T, times), (R, rows), (C, cols), (L, l_j), (V, v_j), (B, base)):
            all_s[f, at] = value
        return carry

    lax.fori_loop(0, runs, fields, 0)

    def clear(k, carry):
        for ref, first, size in ((x_s, 8, M_ROWS), (a_buf, 0, a_buf.shape[0]), (b_buf, 0, b_buf.shape[0])):
            at = pl.ds(pl.multiple_of(first + k * (size // 4), 8), size // 4)
            ref[at] = jnp.zeros((size // 4, ref.shape[1]), ref.dtype)
        return carry

    lax.fori_loop(0, 4, clear, 0)
    pad = (tall, events)
    start = jnp.broadcast_to(g_ref[0, 0, 0:1, 0:1], pad)
    zeros = jnp.zeros(pad, f32)
    for f, value in ((T, start), (R, zeros), (C, zeros), (L, jnp.full(pad, -1e30, f32)), (V, zeros)):
        all_s[f, blocks : blocks + tall] = value

    need_f = all_s[PICK, 0:blocks]
    upper = lax.broadcasted_iota(i32, (events, events), 0) <= lax.broadcasted_iota(
        i32, (events, events), 1
    )
    upper = jnp.where(upper, 1.0, 0.0).astype(bf16)
    pos = jnp.dot(need_f.astype(bf16), upper, preferred_element_type=f32)
    all_s[RANK, 0:blocks] = pos
    all_s[PICK, 0:blocks] = need_f * pos

    def row_of(b):
        def part(field, h):
            return all_s[field, pl.ds(b, 1), :][:, h * LANES : (h + 1) * LANES]

        return part

    def lane_sums(t_i, r_i, c_i, b, before):
        total = None
        for back in range(NB + 1):
            part = row_of(b if back == 0 else jnp.where(b >= back, b - back, blocks))
            for h in range(halves):
                gap = (t_i - part(T, h)) + omori_offset
                dr = r_i - part(R, h)
                dc = c_i - part(C, h)
                expo = (part(L, h) - (omori_power * LOG2E) * jnp.log(gap)) - (
                    dr * dr + dc * dc
                ) * part(V, h)
                term = jnp.exp2(expo)
                if back == 0:
                    term = jnp.where(before(part, h), term, 0.0)
                total = term if total is None else total + term
        return jnp.sum(total, axis=1, keepdims=True)

    sub_f = lax.broadcasted_iota(i32, (UNIT, LANES), 0).astype(f32)
    lane_f = lax.broadcasted_iota(i32, (UNIT, LANES), 1).astype(f32)
    own_rows = jnp.concatenate(
        [
            g_ref[own % SPLIT, own // SPLIT, 0:1, k * events : (k + 1) * events]
            for k in range(3)
        ]
        + [jnp.zeros((5, events), f32)]
    )
    own_cols = jnp.transpose(own_rows)
    for k in range(3):
        own_s[k] = jnp.broadcast_to(own_cols[:, k : k + 1], (events, LANES))

    dep_s[2] = jnp.zeros_like(dep_s[2])

    for copy in copies:
        copy.wait()
    total_units = (listed - 1) - ((fst_s[0, listed - 1] - beyond) * (1.0 / UNIT)).astype(i32)

    rank = sub_f + 1.0
    slots = STEP * UNIT
    lane_s = lax.broadcasted_iota(i32, (slots, LANES), 1)
    m_row = (lane_s % LATITUDE_SPAN).astype(f32)
    col_blocks = M_ROWS // LATITUDE_SPAN
    m_hi = []
    for h in range(M_ROWS // LANES):
        m = lane_s + h * LANES
        m_hi.append((m // LATITUDE_SPAN % 2 * (col_blocks // 2) + m // (2 * LATITUDE_SPAN)).astype(FT))
    l_lo = [(lane_s + h * LANES).astype(FT) for h in range(LO_COLS // LANES)]
    zero, one = jnp.zeros((), FT), jnp.ones((), FT)

    def flush(size):
        x_s[8 : 8 + M_ROWS] += lax.dot_general(
            a_buf[0:size], b_buf[0:size], (((0,), (0,)), ((), ())), preferred_element_type=f32
        )

    def factors(slot):
        r_i, c_i, b_i, trig = dep_s[0], dep_s[1], dep_s[2], dep_s[3]
        share = jnp.where(b_i > 0.0, b_i / (b_i + trig), 0.0)
        share = share.astype(bf16).astype(f32)
        hi = jnp.floor(c_i * (1.0 / LO_COLS))
        lo = (c_i - hi * LO_COLS).astype(FT)
        hi = hi.astype(FT)
        d = m_row - (r_i - first_row)
        d2 = d * d
        w = jnp.exp2(d2 * (-LOG2E / (2.0 * smooth_sigma**2))) * share
        w = jnp.where(d2 < (rim_width + 0.5) ** 2, w, 0.0).astype(FT)
        at = slice(slot * slots, (slot + 1) * slots)
        for h in range(M_ROWS // LANES):
            a_buf[at, h * LANES : (h + 1) * LANES] = jnp.where(m_hi[h] == hi, w, zero).astype(bf16)
        for h in range(LO_COLS // LANES):
            b_buf[at, h * LANES : (h + 1) * LANES] = jnp.where(l_lo[h] == lo, one, zero).astype(bf16)

    def unit_triggers(i):
        for j in range(STEP):
            u = i * STEP + j
            b = blk_s[0, u]
            order = rank + fst_s[0, u]
            at = slice(j * UNIT, (j + 1) * UNIT)
            t_i, r_i, c_i = sel_s[0, at], sel_s[1, at], sel_s[2, at]
            trig = lane_sums(t_i, r_i, c_i, b, lambda part, h: part(RANK, h) < order)
            dep_s[0, at] = r_i
            dep_s[1, at] = c_i
            dep_s[2, at] = sel_s[3, at]
            dep_s[3, at] = jnp.broadcast_to(trig, (UNIT, LANES))

    def pick_events(i):
        for j in range(STEP):
            u = i * STEP + j
            b = blk_s[0, u]
            order = rank + fst_s[0, u]
            part = row_of(b)
            picks = [part(PICK, h) == order for h in range(halves)]
            for k, field in enumerate((T, R, C, B)):
                value = None
                for h in range(halves):
                    piece = jnp.where(picks[h], part(field, h), 0.0)
                    value = piece if value is None else value + piece
                value = jnp.sum(value, axis=1, keepdims=True)
                sel_s[k, j * UNIT : (j + 1) * UNIT] = jnp.broadcast_to(value, (UNIT, LANES))

    total_steps = (total_units + (STEP - 1)) // STEP
    pick_events(0)

    def step(i, carry):
        flush(slots)
        factors(0)
        unit_triggers(i)
        pick_events(i + 1)
        return carry

    lax.fori_loop(0, total_steps, step, 0)
    factors(1)
    flush(2 * slots)

    span = LATITUDE_SPAN
    wide = LO_COLS // LANES
    middle = (col_blocks // 2) * LO_COLS
    edge = jnp.zeros((span, LO_COLS), f32)
    x_s[0:8] = jnp.concatenate([edge, x_s[M_ROWS : M_ROWS + span]])
    x_s[8 + M_ROWS : 16 + M_ROWS] = jnp.concatenate([x_s[8 + span : 16], edge])
    lane_t = lax.broadcasted_iota(i32, (8, LANES), 1)
    per = M_ROWS // (8 * FINAL)
    own_per = events // (UNIT * FINAL)

    def rows_at(at):
        return slice(at, at + UNIT) if isinstance(at, int) else pl.ds(pl.multiple_of(at, UNIT), UNIT)

    def columns(g, carry):
        for p in range(per):
            for j in range(p * own_per // per, (p + 1) * own_per // per):
                at = g * (own_per * UNIT) + j * UNIT
                target = sub_f + float(at) if isinstance(at, int) else sub_f + at.astype(f32)
                t_i, r_i, c_i = (own_s[n, rows_at(at)] for n in range(3))
                trig = lane_sums(t_i, r_i, c_i, own, lambda part, h: lane_f + h * LANES < target)
                own_s[3, rows_at(at)] = jnp.broadcast_to(trig, (UNIT, LANES))
            m = g * (8 * per) + 8 * p

            def tile(shift, h):
                return x_s[rows_at(m + 8 + shift), h * LANES : (h + 1) * LANES]

            mids = [tile(0, h) for h in range(wide)]
            lefts = [tile(-8, wide - 1)] + mids[:-1]
            rights = mids[1:] + [tile(8, 0)]
            for h in range(wide):
                acc = mids[h] * (WEIGHTS[rim_width] / WEIGHT_SUM**2)
                for b in range(1, rim_width + 1):
                    from_left = pltpu.roll(jnp.where(lane_t >= LANES - b, lefts[h], mids[h]), b, 1)
                    from_right = pltpu.roll(jnp.where(lane_t < b, rights[h], mids[h]), LANES - b, 1)
                    acc = acc + (from_left + from_right) * (WEIGHTS[rim_width + b] / WEIGHT_SUM**2)
                at = (g * per + p) * LO_COLS + h * LANES
                for half in range(2):
                    place = at + half * middle
                    place = slice(place, place + LANES) if isinstance(place, int) else pl.ds(pl.multiple_of(place, LANES), LANES)
                    dens_ref[:, place] = acc[half * span : (half + 1) * span]
        return carry

    if FINAL == 1:
        columns(0, 0)
    else:
        lax.fori_loop(0, FINAL, columns, 0)
    for h in range(halves):
        found = own_s[3, h * LANES : (h + 1) * LANES]
        diagonal = lax.broadcasted_iota(i32, (LANES, LANES), 0) == lax.broadcasted_iota(
            i32, (LANES, LANES), 1
        )
        trig = jnp.sum(jnp.where(diagonal, found, 0.0), axis=0, keepdims=True)
        logint_ref[:, h * LANES : (h + 1) * LANES] = jnp.log(row_of(own)(B, h) + trig)


def body(times, cell_row, cell_col, magnitude, base_rate, productivity, spread):
    events = times.shape[0]
    blocks = lax.axis_size(AXES)
    f32 = jnp.float32
    rows = [x.reshape(1, events) for x in (times, cell_row, cell_col, magnitude, base_rate)]
    vmem = pl.BlockSpec(memory_space=pltpu.VMEM)
    rows += [x.reshape(1, -1) for x in (productivity, spread)]
    table = jax.ShapeDtypeStruct((1, productivity.shape[0]), f32)
    spread_out, l_table, v_table = pl.pallas_call(
        spread_kernel,
        out_shape=(jax.ShapeDtypeStruct((blocks, 1, 5 * events), f32), table, table),
        in_specs=[vmem] * 7,
        out_specs=(vmem, vmem, vmem),
        compiler_params=pltpu.CompilerParams(vmem_limit_bytes=16 * MIB),
    )(*rows)
    runs = blocks // SPLIT
    order = [r + SPLIT * q for r in range(SPLIT) for q in range(runs)]
    gathered = lax.all_to_all(
        spread_out, AXES, 0, 0, tiled=True, axis_index_groups=[order]
    ).reshape(SPLIT, runs, 1, 5 * events)
    listed = blocks * events // UNIT + LANES
    log_intensity, density = pl.pallas_call(
        kernel,
        out_shape=(
            jax.ShapeDtypeStruct((1, events), f32),
            jax.ShapeDtypeStruct((LATITUDE_SPAN, COLS), f32),
        ),
        in_specs=[vmem, vmem, vmem],
        out_specs=(vmem, vmem),
        scratch_shapes=[
            pltpu.VMEM((FIELDS, blocks + 8, events), f32),
            pltpu.VMEM((4, events, LANES), f32),
            pltpu.VMEM((1, listed), jnp.int32),
            pltpu.VMEM((1, listed), f32),
            pltpu.SMEM((1, listed), jnp.int32),
            pltpu.SMEM((1, listed), f32),
            pltpu.VMEM((4, STEP * UNIT, LANES), f32),
            pltpu.VMEM((4, STEP * UNIT, LANES), f32),
            pltpu.VMEM((2 * STEP * UNIT, M_ROWS), jnp.bfloat16),
            pltpu.VMEM((2 * STEP * UNIT, LO_COLS), jnp.bfloat16),
            pltpu.VMEM((M_ROWS + 16, LO_COLS), f32),
            pltpu.SemaphoreType.DMA((2,)),
        ],
        compiler_params=pltpu.CompilerParams(vmem_limit_bytes=32 * MIB),
    )(gathered, l_table, v_table)
    return (log_intensity.reshape(events), density)


def solution(mesh):
    in_specs = (P(AXES), P(AXES), P(AXES), P(AXES), P(AXES), P(), P())
    out_specs = (P(AXES), P(AXES, None))
    return jax.shard_map(body, mesh=mesh, in_specs=in_specs, out_specs=out_specs, check_vma=False)
```
